256 devices in a mesh: half: 2 (over y_lo), shard: 128 (over y_hi, z, x, core).
Axes of the slice: x: 4, y: 4 (y_hi: 2, y_lo: 2; y = y_hi * 2 + y_lo), z: 8, core: 2. Of those that a mesh axis runs over, the one named last changes fastest.
Arguments:
- recording: float32 [32, 2048, 1024], P('half', 'shard'), may hold values from -600 to 600
- source_channels: int32 [256], replicated, may hold values from 0 to 2047, as said below
Outputs:
- correlations: float32 [256, 2048, 512], P('half', 'shard')
The draws below stay inside these ranges and needn't reach their ends.
Inputs may be any that keep to these rules, and one draw needn't show every extreme that they name: `source_channels`: distinct channel indices.
All inputs are finite; a program needn't handle non-finite values.
Results may differ from the reference program's by a relative error of at most 0.000071.
Values sent between devices are 32-bit elements; how exact they have to be, the bound alone decides.
A program may use at most 64 MiB of HBM per device.

```python
import jax
import jax.numpy as jnp
from jax import lax

C = 2048
L = 1024
F = 128
LAGS = 512
SMOOTH = 2
NSRC = 256
SEG = 32


def draw_recording(key, part):
    base = jax.random.fold_in(key, 11)
    key_chan, key_seg, key_noise = jax.random.split(base, 3)
    chan_gain = jnp.exp(jax.random.uniform(key_chan, (1, C, 1), jnp.float32) * jnp.log(10.0))
    seg_gain = jnp.exp(jax.random.uniform(key_seg, (SEG, 1, 1), jnp.float32) * jnp.log(10.0))
    signal = jnp.clip(jax.random.normal(key_noise, (SEG, C, L), jnp.float32), -6.0, 6.0)
    return (signal * chan_gain * seg_gain).astype(jnp.float32)


def draw_source_channels(key, part):
    base = jax.random.fold_in(key, 23)
    key_pick, key_order = jax.random.split(base, 2)
    inner = jax.random.permutation(key_pick, C - 2)[:NSRC - 2] + 1
    chosen = jnp.concatenate((inner.astype(jnp.int32), jnp.array([0, C - 1], dtype=jnp.int32)))
    order = jax.random.permutation(key_order, NSRC)
    return chosen[order].astype(jnp.int32)


def setup_inputs(seed: int = 0) -> dict:
    streams_of = jax.random.split(jax.random.key(seed), 3)
    recording = draw_recording(jax.random.fold_in(streams_of[2], 71), 0)
    source_channels = draw_source_channels(jax.random.fold_in(streams_of[2], 71), 0)
    return {"recording": recording, "source_channels": source_channels}


water_level = 0.2
epsilon = 1e-05

def forward_table(samples, freq_count):
    bins = jnp.arange(freq_count, dtype=jnp.int32) + 1
    times = jnp.arange(samples, dtype=jnp.int32)
    phase = bins[:, None] * times[None, :] % samples
    angle = 2.0 * jnp.pi * phase.astype(jnp.float32) / samples
    taper = 0.5 - 0.5 * jnp.cos(2.0 * jnp.pi * times.astype(jnp.float32) / samples)
    return jnp.stack((jnp.cos(angle) * taper[None, :], -jnp.sin(angle) * taper[None, :]), axis=1)

def inverse_table(samples, freq_count, lag_count, segments):
    bins = jnp.arange(freq_count, dtype=jnp.int32) + 1
    shifts = jnp.arange(lag_count, dtype=jnp.int32) - lag_count // 2
    phase = bins[:, None] * shifts[None, :] % samples
    angle = 2.0 * jnp.pi * phase.astype(jnp.float32) / samples
    scale = 1.0 / jnp.sqrt(jnp.float32(segments * freq_count))
    return jnp.stack((jnp.cos(angle) * scale, -jnp.sin(angle) * scale), axis=1)

def whiten(spectra):
    magnitude = jnp.sqrt(spectra[:, 0] * spectra[:, 0] + spectra[:, 1] * spectra[:, 1])
    freq_count = magnitude.shape[0]
    padded = jnp.pad(magnitude, ((SMOOTH, SMOOTH), (0, 0), (0, 0)))
    smoothed = padded[0:freq_count]
    for offset in range(1, 2 * SMOOTH + 1):
        smoothed = smoothed + padded[offset:offset + freq_count]
    smoothed = smoothed / (2 * SMOOTH + 1)
    water_mark = lax.optimization_barrier(jnp.mean(magnitude, axis=0, keepdims=True))
    divisor = smoothed + water_level * water_mark + epsilon
    return spectra / divisor[:, None]

def correlate(whitened, indices):
    sources = jnp.take(whitened, indices, axis=2)
    src_real, src_imag = (sources[:, 0], sources[:, 1])
    rec_real, rec_imag = (whitened[:, 0], whitened[:, 1])
    high = lax.Precision.HIGHEST
    cross_real = jnp.einsum('fnx,fcx->fnc', src_real, rec_real, precision=high) + jnp.einsum('fnx,fcx->fnc', src_imag, rec_imag, precision=high)
    cross_imag = jnp.einsum('fnx,fcx->fnc', src_real, rec_imag, precision=high) - jnp.einsum('fnx,fcx->fnc', src_imag, rec_real, precision=high)
    return jnp.stack((cross_real, cross_imag), axis=1)

def reference(recording, source_channels):
    forward = forward_table(L, F)
    spectra = jnp.einsum('fqt,sct->fqcs', forward, recording, precision=lax.Precision.HIGHEST)
    whitened = whiten(spectra)
    cross = correlate(whitened, source_channels)
    backward = inverse_table(L, F, LAGS, SEG)
    return jnp.einsum('fqnc,fql->ncl', cross, backward, precision=lax.Precision.HIGHEST)
```

```python
import functools

import jax
import jax.numpy as jnp
import numpy as np
from jax import lax
from jax.experimental import pallas as pl
from jax.experimental.pallas import tpu as pltpu
from jax.sharding import PartitionSpec as P

F = 128
L = 1024
LAGS = 512
SEG = 32
water_level = 0.2
epsilon = 1e-05

NX, NZ = 4, 8
NJ = 64
ANY = pl.BlockSpec(memory_space=pl.ANY)
VMEM = pl.BlockSpec(memory_space=pltpu.VMEM)
SMEM = pl.BlockSpec(memory_space=pltpu.SMEM)
MESH = pl.DeviceIdType.MESH
BF = jnp.bfloat16
F32 = jnp.float32


def split_np(table):
    hi = table.astype(np.float32).astype(jnp.bfloat16)
    lo = (table - hi.astype(np.float64)).astype(np.float32).astype(jnp.bfloat16)
    return hi, lo


def forward_table():
    bins = np.arange(F) + 1
    times = np.arange(L)
    angle = 2.0 * np.pi * (bins[:, None] * times[None, :] % L) / L
    taper = 0.5 - 0.5 * np.cos(2.0 * np.pi * times / L)
    return np.concatenate((np.cos(angle) * taper, -np.sin(angle) * taper), axis=0)


def inverse_table():
    bins = np.arange(F) + 1
    shifts = np.arange(LAGS) - LAGS // 2
    angle = 2.0 * np.pi * (bins[:, None] * shifts[None, :] % L) / L
    return np.concatenate((np.cos(angle), -np.sin(angle)), axis=0) / np.sqrt(SEG * F)


def split(v):
    hi = v.astype(BF)
    return hi, (v - hi.astype(F32)).astype(BF)


def dot(a, b, ca, cb):
    return lax.dot_general(a, b, (((ca,), (cb,)), ((), ())), preferred_element_type=F32)


def whiten_kernel(rec_ref, hi_ref, lo_ref, out_ref):
    rec_hi, rec_lo = split(rec_ref[...])
    spec = dot(hi_ref[...], rec_hi, 1, 1) + dot(hi_ref[...], rec_lo, 1, 1) + dot(lo_ref[...], rec_hi, 1, 1)
    re, im = spec[:F], spec[F:]
    mag = jnp.sqrt(re * re + im * im)
    zeros = jnp.zeros((2, mag.shape[1]), F32)
    pad = jnp.concatenate((zeros, mag, zeros), axis=0)
    smooth = pad[0:F]
    for off in range(1, 5):
        smooth = smooth + pad[off : off + F]
    mean = jnp.sum(mag, axis=0, keepdims=True) * (1.0 / F)
    divisor = smooth / 5.0 + water_level * mean + epsilon
    for q, part in enumerate((re, im)):
        white = part / divisor
        for s_hi in range(2):
            out_ref[pl.ds(2 * q + s_hi, F, stride=4), :] = white[:, 128 * s_hi : 128 * (s_hi + 1)]


def events():
    out = []
    for dz in (0, 1, -1, 2, -2, 3, -3, 4):
        for dx in (0, 1, -1, 2):
            if (dz, dx) == (0, 0):
                continue
            az, ax = abs(dz), abs(dx)
            out.append((1.0 * ax + 2.0 * az * (1.0 if ax == 0 else 1.2) + 0.3 * ax, 0, dz, dx))
            out.append((1.0 * az + 2.0 * ax + (0.5 if ax else 0), 1, dz, dx))
    out.sort(key=lambda e: e[0])
    return [e[1:] for e in out]


def comm_kernel(idx_ref, w_ref, g_ref, wo_ref, a_ref, gm_ref, pick_ref, y_ref,
                a_send, a_recv, y_send, y_recv, wo_send, wo_recv, g_send, g_recv, sib_recv):
    h = lax.axis_index("half")
    s = lax.axis_index("shard")
    yh, j = s // NJ, s % NJ
    z, x, k = j // 8, (j // 2) % 4, j % 2

    barrier = pltpu.get_barrier_semaphore()

    def greet(i, carry):
        pl.semaphore_signal(barrier, inc=1, device_id=(h, yh * NJ + (j + i) % NJ), device_id_type=MESH)
        return carry

    lax.fori_loop(1, NJ, greet, 0)
    ring_y = [(h, (1 - yh) * NJ + j), (1 - h, yh * NJ + j), (1 - h, (1 - yh) * NJ + j)]
    for dev in ring_y:
        pl.semaphore_signal(barrier, inc=1, device_id=dev, device_id_type=MESH)
    pl.semaphore_wait(barrier, NJ + 2)

    def remote(src, dst, ssem, rsem, dev):
        return pltpu.make_async_remote_copy(
            src_ref=src, dst_ref=dst, send_sem=ssem, recv_sem=rsem, device_id=dev, device_id_type=MESH
        )

    def scatter(i, carry):
        t = (j + i) % NJ
        remote(w_ref.at[t], a_ref.at[j], a_send, a_recv, (h, yh * NJ + t)).start()
        return carry

    lax.fori_loop(1, NJ, scatter, 0)
    wo = remote(w_ref, wo_ref, wo_send, wo_recv, ring_y[1])
    wo.start()
    a_ref[j] = w_ref[j]
    all_a = remote(w_ref.at[pl.ds(0, NJ - 1)], a_ref.at[pl.ds(0, NJ - 1)], a_send, a_recv, ring_y[0])
    all_a.wait_send()
    all_a.wait_recv()

    lane_c = lax.broadcasted_iota(jnp.int32, (8, 128), 1) & 15

    def pick(n, carry):
        q = idx_ref[n]
        p = q >> 4
        c = jnp.where((p >> 6) == yh, q & 15, 99)
        v = jnp.where(lane_c == c, a_ref[p & (NJ - 1)], 0.0)
        gm_ref[pl.ds(n, 8, stride=256), :] = v
        return carry

    lax.fori_loop(0, 256, pick, 0, unroll=8)
    row = lax.broadcasted_iota(jnp.int32, (8, 128), 0)
    col = lax.broadcasted_iota(jnp.int32, (8, 128), 1)
    fold = jnp.where((col >> 4) == row, 1.0, 0.0).astype(BF)
    for e in range(8):
        v = gm_ref[256 * e : 256 * (e + 1), :]
        hi = v.astype(BF)
        rest = v - hi.astype(F32)
        mid = rest.astype(BF)
        lo = (rest - mid.astype(F32)).astype(BF)
        got = dot(fold, hi, 1, 1) + dot(fold, mid, 1, 1) + dot(fold, lo, 1, 1)
        pick_ref[0, 8 * e : 8 * (e + 1), :] = got[:, :128]
        pick_ref[1, 8 * e : 8 * (e + 1), :] = got[:, 128:]

    trades = [
        remote(pick_ref.at[h], y_ref.at[0], y_send.at[0], y_recv.at[0], ring_y[0]),
        remote(pick_ref.at[1 - h], y_ref.at[1], y_send.at[1], y_recv.at[1], ring_y[1]),
        remote(pick_ref.at[1 - h], y_ref.at[2], y_send.at[2], y_recv.at[2], ring_y[2]),
    ]
    for t in trades:
        t.start()
    for t in trades:
        t.wait()
    own = pick_ref[h] + y_ref[0]
    other = y_ref[1] + y_ref[2]
    for f2 in range(2):
        g_ref[j, f2, 0] = own[32 * f2 : 32 * f2 + 32]
        g_ref[j, f2, 1] = other[32 * f2 : 32 * f2 + 32]

    def place(dz, dx):
        return ((z + dz + NZ) % NZ) * 8 + ((x + dx + NX) % NX) * 2 + k

    def send(b, f2, dz, dx):
        blk = g_ref.at[b, f2]
        remote(blk, blk, g_send, g_recv.at[b, f2], (h, yh * NJ + place(dz, dx))).start()

    def share(b, f2):
        blk = g_ref.at[b, f2]
        remote(blk, blk, g_send, sib_recv, (h, s + 1 - 2 * k)).start()

    for dx in (1, -1, 2):
        send(j, 0, 0, dx)
    for dz in (1, -1):
        send(j, 0, dz, 0)
    for dx in (1, -1):
        send(j, 1, 0, dx)
    for dz in (1, -1, 2, -2, 3, -3, 4):
        send(j, 1, dz, 0)
    share(j, 0)
    share(j, 1)
    for f2, dz, dx in events():
        b = place(dz, dx)
        blk = g_ref.at[b, f2]
        remote(blk, blk, g_send, g_recv.at[b, f2], ring_y[0]).wait_recv()
        if f2 == 0:
            xs = (x + dx + NX) % NX
            if dz == 0:
                send(b, 0, 1, 0)
                send(b, 0, -1, 0)
            elif dz in (-1, -2):
                send(b, 0, 1, 0)
            elif dz in (1, 2):
                send(b, 0, -1, 0)
            elif dz == -3:
                @pl.when(xs % 2 == 0)
                def _():
                    send(b, 0, 1, 0)
            elif dz == 3:
                @pl.when(xs % 2 == 1)
                def _():
                    send(b, 0, -1, 0)
        else:
            zs = (z + dz + NZ) % NZ
            if dx == 0:
                send(b, 1, 0, 1)
                send(b, 1, 0, -1)
            elif dx == -1:
                @pl.when(zs % 2 == 0)
                def _():
                    send(b, 1, 0, 1)
            elif dx == 1:
                @pl.when(zs % 2 == 1)
                def _():
                    send(b, 1, 0, -1)
        share(b, f2)
    half_g = g_ref.at[pl.ds(0, NJ // 2)]
    remote(half_g, half_g, g_send, sib_recv, ring_y[0]).wait_recv()
    most_g = g_ref.at[pl.ds(0, NJ - 1)]
    remote(most_g, most_g, g_send, sib_recv, ring_y[0]).wait_send()
    wo.wait()


def output_kernel(g_ref, w_ref, wo_ref, hi_ref, lo_ref, out_ref, lhs_ref, x_ref, xt_ref, stage_ref, sem):
    lane = lax.broadcasted_iota(jnp.int32, (16, 128), 1)
    parts = []
    for ref in (w_ref, wo_ref):
        for e in range(4):
            parts.append(ref[pl.ds(e, F, stride=4), :].T)
    v = [parts[i // 8][16 * (i % 8) : 16 * (i % 8) + 16, :] for i in range(64)]
    for bit in range(6):
        step = 1 << bit
        low = (lane & step) == 0
        for i in range(64):
            if i & step:
                continue
            a, b = v[i], v[i + step]
            v[i] = jnp.where(low, a, pltpu.roll(b, step, 1))
            v[i + step] = jnp.where(low, pltpu.roll(a, 128 - step, 1), b)
    first = (lane & 16) == 0
    top = lane < 64
    for g in range(64):
        a = v[g]
        b = jnp.where(first, pltpu.roll(a, 112, 1), -pltpu.roll(a, 16, 1))
        rows = []
        for r in (a, b):
            rows.append(jnp.where(top, r, 0.0))
            rows.append(jnp.where(top, 0.0, r))
        m = jnp.concatenate(rows, axis=0)
        hi, lo = split(m)
        lhs_ref[g] = jnp.concatenate((hi, lo), axis=0)

    def cross(g, carry):
        src = jnp.concatenate((g_ref[g], g_ref[g + 64]), axis=0)
        hi, lo = split(src)
        res = dot(lhs_ref[g], jnp.concatenate((hi, lo), axis=1), 1, 0)
        res = res[:64, :128] + (res[:64, 128:] + res[64:, :128])
        for i in range(4):
            x_ref[pl.ds(64 * i + g, 16, stride=256), :] = res[16 * i : 16 * i + 16]
        return carry

    lax.fori_loop(0, 64, cross, 0, unroll=4)
    copies = []
    for half in range(2):
        th = hi_ref[:, 256 * half : 256 * half + 256]
        tl = lo_ref[:, 256 * half : 256 * half + 256]
        for c in range(16):
            if half == 0:
                hi, lo = split(x_ref[256 * c : 256 * c + 256, :].T)
                xt_ref[0, c], xt_ref[1, c] = hi, lo
            hi, lo = xt_ref[0, c], xt_ref[1, c]
            res = dot(hi, th, 1, 0) + dot(hi, tl, 1, 0) + dot(lo, th, 1, 0)
            for b in range(2):
                stage_ref[2 * half + b, pl.ds(c, 128, stride=16), :] = res[:, 128 * b : 128 * b + 128]
        for b in range(2 * half, 2 * half + 2):
            copy = pltpu.make_async_copy(stage_ref.at[b], out_ref.at[:, pl.ds(128 * b, 128)], sem.at[b])
            copy.start()
            copies.append(copy)
    for copy in copies:
        copy.wait()


def body(recording, source_channels):
    fwd_hi, fwd_lo = (jnp.asarray(t) for t in split_np(forward_table()))
    inv_hi, inv_lo = (jnp.asarray(t) for t in split_np(inverse_table()))
    rec = recording.reshape(256, L)
    w = pl.pallas_call(
        whiten_kernel,
        out_shape=jax.ShapeDtypeStruct((512, 128), F32),
        in_specs=[VMEM] * 3,
        out_specs=VMEM,
        name="whiten",
    )(rec, fwd_hi, fwd_lo)
    dma = pltpu.SemaphoreType.DMA
    g, wo = pl.pallas_call(
        comm_kernel,
        out_shape=(
            jax.ShapeDtypeStruct((NJ, 2, 2, 32, 128), F32),
            jax.ShapeDtypeStruct((NJ, 8, 128), F32),
        ),
        in_specs=[SMEM, VMEM],
        out_specs=(VMEM, VMEM),
        scratch_shapes=[
            pltpu.VMEM((NJ, 8, 128), F32),
            pltpu.VMEM((2048, 128), F32),
            pltpu.VMEM((2, 64, 128), F32),
            pltpu.VMEM((3, 64, 128), F32),
            dma, dma, dma((3,)), dma((3,)), dma, dma, dma, dma((NJ, 2)), dma,
        ],
        compiler_params=pltpu.CompilerParams(collective_id=0, has_side_effects=True),
        name="exchange",
    )(source_channels, w.reshape(NJ, 8, 128))
    out = pl.pallas_call(
        output_kernel,
        out_shape=jax.ShapeDtypeStruct((128 * 16, LAGS), F32),
        in_specs=[VMEM] * 5,
        out_specs=ANY,
        scratch_shapes=[
            pltpu.VMEM((64, 128, 128), BF),
            pltpu.VMEM((16 * 256, 128), F32),
            pltpu.VMEM((2, 16, 128, 256), BF),
            pltpu.VMEM((4, 2048, 128), F32),
            dma((4,)),
        ],
        name="correlate",
    )(g.reshape(F, 64, 128), w, wo.reshape(512, 128), inv_hi, inv_lo)
    return out.reshape(128, 16, LAGS)


def solution(mesh):
    return jax.shard_map(
        body,
        mesh=mesh,
        in_specs=(P("half", "shard", None), P()),
        out_specs=P("half", "shard", None),
        check_vma=False,
    )
```

```python
import functools

import jax
import jax.numpy as jnp
import numpy as np
from jax import lax
from jax.experimental import pallas as pl
from jax.experimental.pallas import tpu as pltpu
from jax.sharding import PartitionSpec as P

F = 128
L = 1024
LAGS = 512
SEG = 32
water_level = 0.2
epsilon = 1e-05

NX, NZ = 4, 8
NJ = 64
ANY = pl.BlockSpec(memory_space=pl.ANY)
VMEM = pl.BlockSpec(memory_space=pltpu.VMEM)
SMEM = pl.BlockSpec(memory_space=pltpu.SMEM)
MESH = pl.DeviceIdType.MESH
BF = jnp.bfloat16
F32 = jnp.float32


def split_np(table):
    hi = table.astype(np.float32).astype(jnp.bfloat16)
    lo = (table - hi.astype(np.float64)).astype(np.float32).astype(jnp.bfloat16)
    return hi, lo


def forward_table():
    bins = np.arange(F) + 1
    times = np.arange(L)
    angle = 2.0 * np.pi * (bins[:, None] * times[None, :] % L) / L
    taper = 0.5 - 0.5 * np.cos(2.0 * np.pi * times / L)
    return np.concatenate((np.cos(angle) * taper, -np.sin(angle) * taper), axis=0)


def inverse_table():
    bins = np.arange(F) + 1
    shifts = np.arange(LAGS) - LAGS // 2
    angle = 2.0 * np.pi * (bins[:, None] * shifts[None, :] % L) / L
    return np.concatenate((np.cos(angle), -np.sin(angle)), axis=0) / np.sqrt(SEG * F)


def split(v):
    hi = v.astype(BF)
    return hi, (v - hi.astype(F32)).astype(BF)


def dot(a, b, ca, cb):
    return lax.dot_general(a, b, (((ca,), (cb,)), ((), ())), preferred_element_type=F32)


OFF_Z = (1, -1, 2, -2, 3, -3, 4)


def events():
    out = []
    for dz in (0,) + OFF_Z:
        for dx in (0, 1, -1, 2):
            if (dz, dx) == (0, 0):
                continue
            az, ax = abs(dz), abs(dx)
            out.append((1.0 * ax + 2.0 * az * (1.0 if ax == 0 else 1.2) + 0.3 * ax, 0, dz, dx))
            out.append((1.0 * az + 2.0 * ax + (0.5 if ax else 0), 1, dz, dx))
    out.sort(key=lambda e: e[0])
    return [e[1:] for e in out]


def whiten(rec_ref, hi_ref, lo_ref, out_ref):
    rec_hi, rec_lo = split(rec_ref[...])
    spec = dot(hi_ref[...], rec_hi, 1, 1) + dot(hi_ref[...], rec_lo, 1, 1) + dot(lo_ref[...], rec_hi, 1, 1)
    re, im = spec[:F], spec[F:]
    mag = jnp.sqrt(re * re + im * im)
    zeros = jnp.zeros((2, mag.shape[1]), F32)
    pad = jnp.concatenate((zeros, mag, zeros), axis=0)
    smooth = pad[0:F]
    for off in range(1, 5):
        smooth = smooth + pad[off : off + F]
    mean = jnp.sum(mag, axis=0, keepdims=True) * (1.0 / F)
    divisor = smooth / 5.0 + water_level * mean + epsilon
    for q, part in enumerate((re, im)):
        white = part / divisor
        for s_hi in range(2):
            out_ref[pl.ds(2 * q + s_hi, F, stride=4), :] = white[:, 128 * s_hi : 128 * (s_hi + 1)]


def swap(v, bit, lane):
    step = 1 << bit
    low = (lane & step) == 0
    v = list(v)
    for i in range(len(v)):
        if i & step:
            continue
        a, b = v[i], v[i + step]
        v[i] = jnp.where(low, a, pltpu.roll(b, step, 1))
        v[i + step] = jnp.where(low, pltpu.roll(a, 128 - step, 1), b)
    return v


def lanes():
    return lax.broadcasted_iota(jnp.int32, (16, 128), 1)


def receivers_first(ref, mid_ref, side):
    v = []
    for e in range(4):
        t = ref[pl.ds(e, F, stride=4), :].T
        v += [t[16 * i : 16 * i + 16] for i in range(8)]
    for bit in range(5):
        v = swap(v, bit, lanes())
    for i in range(32):
        mid_ref[side, i] = v[i]


def receivers_last(mid_ref, lhs_ref):
    lane = lanes()
    first = (lane & 16) == 0
    top = lane < 64
    low = (lane & 32) == 0
    for i in range(32):
        a, b = mid_ref[0, i], mid_ref[1, i]
        pair = (jnp.where(low, a, pltpu.roll(b, 32, 1)), jnp.where(low, pltpu.roll(a, 96, 1), b))
        for half in range(2):
            a = pair[half]
            b = jnp.where(first, pltpu.roll(a, 112, 1), -pltpu.roll(a, 16, 1))
            rows = []
            for r in (a, b):
                rows.append(jnp.where(top, r, 0.0))
                rows.append(jnp.where(top, 0.0, r))
            hi, lo = split(jnp.concatenate(rows, axis=0))
            lhs_ref[32 * half + i] = jnp.concatenate((hi, lo), axis=0)


def exchange_kernel(idx_ref, rec_hbm, hi_hbm, lo_hbm, x_ref, rec_ref, hi_ref, lo_ref, w_ref, wo_ref, z_ref, a_ref,
                    gm_ref, pick_ref, y_ref, g_ref, mid_ref, lhs_ref,
                    load, z_send, z_recv, a_send, a_recv, y_send, y_recv, wo_send, wo_recv, g_send, g_recv):
    h = lax.axis_index("half")
    s = lax.axis_index("shard")
    yh, u, k = s // NJ, (s % NJ) // 2, s % 2
    z, x = u // NX, u % NX
    j = k * 32 + u

    def device(zz, xx, kk):
        return (h, yh * NJ + (zz * NX + xx) * 2 + kk)

    def zat(d):
        return (z + d + NZ) % NZ

    def xat(d):
        return (x + d + NX) % NX

    def remote(src, dst, ssem, rsem, dev):
        return pltpu.make_async_remote_copy(
            src_ref=src, dst_ref=dst, send_sem=ssem, recv_sem=rsem, device_id=dev, device_id_type=MESH
        )

    plane = [(xat(d), kk) for d in (0, 1, -1, 2) for kk in (k, 1 - k)][1:]
    ring_y = [(h, (1 - yh) * NJ + s % NJ), (1 - h, s), (1 - h, (1 - yh) * NJ + s % NJ)]
    barrier = pltpu.get_barrier_semaphore()
    for dev in [device(zat(d), x, k) for d in OFF_Z] + [device(z, *p) for p in plane] + ring_y:
        pl.semaphore_signal(barrier, inc=1, device_id=dev, device_id_type=MESH)
    loads = [
        pltpu.make_async_copy(a, b, load.at[i])
        for i, (a, b) in enumerate(((rec_hbm, rec_ref), (hi_hbm, hi_ref), (lo_hbm, lo_ref)))
    ]
    for c in loads:
        c.start()
    for c in loads:
        c.wait()
    whiten(rec_ref, hi_ref, lo_ref, w_ref)
    pl.semaphore_wait(barrier, 17)

    def rows(kk, zz, n):
        return pl.ds(pl.multiple_of((kk * 32 + zz * NX) * 8, 8), n)

    for d in OFF_Z:
        for kk in range(2):
            remote(
                w_ref.at[rows(kk, zat(d), 32)], z_ref.at[kk, z], z_send, z_recv.at[kk, z], device(zat(d), x, k)
            ).start()
    wo = remote(w_ref, wo_ref, wo_send, wo_recv, ring_y[1])
    wo.start()
    for kk in range(2):
        z_ref[kk, z] = w_ref[rows(kk, z, 32), :]
    receivers_first(w_ref, mid_ref, 0)
    for d in (0,) + OFF_Z:
        zs = zat(d)
        if d:
            for kk in range(2):
                remote(z_ref.at[kk, zs], z_ref.at[kk, zs], z_send, z_recv.at[kk, zs], ring_y[0]).wait_recv()
        mine = k * 32 + zs * NX + x
        for xx, kk in plane:
            src = z_ref.at[kk, zs, pl.ds(pl.multiple_of(xx * 8, 8), 8)]
            remote(src, a_ref.at[mine], a_send, a_recv, device(z, xx, kk)).start()
        a_ref[mine] = z_ref[k, zs, pl.ds(pl.multiple_of(x * 8, 8), 8), :]
    some_a = remote(a_ref.at[pl.ds(0, 56)], a_ref.at[pl.ds(0, 56)], a_send, a_recv, ring_y[0])
    some_a.wait_recv()

    lane_c = lax.broadcasted_iota(jnp.int32, (8, 128), 1) & 15

    def pick(n, carry):
        q = idx_ref[n]
        p = q >> 4
        c = jnp.where((p >> 6) == yh, q & 15, 99)
        v = jnp.where(lane_c == c, a_ref[(p & 1) * 32 + ((p & 63) >> 1)], 0.0)
        gm_ref[pl.ds(n, 8, stride=256), :] = v
        return carry

    lax.fori_loop(0, 256, pick, 0, unroll=8)
    row = lax.broadcasted_iota(jnp.int32, (8, 128), 0)
    col = lax.broadcasted_iota(jnp.int32, (8, 128), 1)
    fold = jnp.where((col >> 4) == row, 1.0, 0.0).astype(BF)
    for e in range(8):
        v = gm_ref[256 * e : 256 * (e + 1), :]
        hi = v.astype(BF)
        rest = v - hi.astype(F32)
        mid = rest.astype(BF)
        lo = (rest - mid.astype(F32)).astype(BF)
        got = dot(fold, hi, 1, 1) + dot(fold, mid, 1, 1) + dot(fold, lo, 1, 1)
        pick_ref[0, 8 * e : 8 * (e + 1), :] = got[:, :128]
        pick_ref[1, 8 * e : 8 * (e + 1), :] = got[:, 128:]

    trades = [
        remote(pick_ref.at[h], y_ref.at[0], y_send.at[0], y_recv.at[0], ring_y[0]),
        remote(pick_ref.at[1 - h], y_ref.at[1], y_send.at[1], y_recv.at[1], ring_y[1]),
        remote(pick_ref.at[1 - h], y_ref.at[2], y_send.at[2], y_recv.at[2], ring_y[2]),
    ]
    for t in trades:
        t.start()
    wo.wait()
    receivers_first(wo_ref, mid_ref, 1)
    receivers_last(mid_ref, lhs_ref)
    for t in trades:
        t.wait()
    own = pick_ref[h] + y_ref[0]
    other = y_ref[1] + y_ref[2]
    for f2 in range(2):
        g_ref[j, f2, 0] = own[32 * f2 : 32 * f2 + 32]
        g_ref[j, f2, 1] = other[32 * f2 : 32 * f2 + 32]

    def send(u2, f2, dz, dx):
        blk = g_ref.at[k * 32 + u2, f2]
        remote(blk, blk, g_send, g_recv.at[k * 32 + u2, f2], device(zat(dz), xat(dx), k)).start()

    def share(u2, f2):
        blk = g_ref.at[k * 32 + u2, f2]
        remote(blk, blk, g_send, g_recv.at[k * 32 + u2, f2], device(z, x, 1 - k)).start()

    def arrived(kk, u2, f2):
        blk = g_ref.at[kk * 32 + u2, f2]
        remote(blk, blk, g_send, g_recv.at[kk * 32 + u2, f2], ring_y[0]).wait_recv()

    def cross(u2, f2):
        arrived(1 - k, u2, f2)
        g = u2 * 2 + f2
        src = jnp.concatenate((g_ref[u2, f2].reshape(64, 128), g_ref[32 + u2, f2].reshape(64, 128)), axis=0)
        hi, lo = split(src)
        res = dot(lhs_ref[g], jnp.concatenate((hi, lo), axis=1), 1, 0)
        res = res[:64, :128] + (res[:64, 128:] + res[64:, :128])
        for i in range(4):
            x_ref[pl.ds(64 * i + g, 16, stride=256), :] = res[16 * i : 16 * i + 16]

    for dx in (1, -1, 2):
        send(u, 0, 0, dx)
    for dz in (1, -1):
        send(u, 0, dz, 0)
    for dx in (1, -1):
        send(u, 1, 0, dx)
    for dz in OFF_Z:
        send(u, 1, dz, 0)
    share(u, 0)
    share(u, 1)
    todo = [(u, 0), (u, 1)]
    for f2, dz, dx in events():
        zs, xs = zat(dz), xat(dx)
        b = zs * NX + xs
        arrived(k, b, f2)
        if f2 == 0:
            if dz == 0:
                send(b, 0, 1, 0)
                send(b, 0, -1, 0)
            elif dz in (-1, -2):
                send(b, 0, 1, 0)
            elif dz in (1, 2):
                send(b, 0, -1, 0)
            elif dz == -3:
                @pl.when(xs % 2 == 0)
                def _():
                    send(b, 0, 1, 0)
            elif dz == 3:
                @pl.when(xs % 2 == 1)
                def _():
                    send(b, 0, -1, 0)
        else:
            if dx == 0:
                send(b, 1, 0, 1)
                send(b, 1, 0, -1)
            elif dx == -1:
                @pl.when(zs % 2 == 0)
                def _():
                    send(b, 1, 0, 1)
            elif dx == 1:
                @pl.when(zs % 2 == 1)
                def _():
                    send(b, 1, 0, -1)
        share(b, f2)
        todo.append((b, f2))
        if len(todo) > 3:
            cross(*todo.pop(0))
    for t in todo:
        cross(*t)
    most_g = g_ref.at[pl.ds(0, NJ - 1)]
    remote(most_g, most_g, g_send, a_recv, ring_y[0]).wait_send()
    some_a.wait_send()
    sent_z = w_ref.at[pl.ds(0, 448)]
    remote(sent_z, sent_z, z_send, a_recv, ring_y[0]).wait_send()


def output_kernel(x_ref, hi_ref, lo_ref, out_ref, xt_ref, stage_ref, sem):
    copies = []
    for half in range(2):
        th = hi_ref[:, 256 * half : 256 * half + 256]
        tl = lo_ref[:, 256 * half : 256 * half + 256]
        for c in range(16):
            if half == 0:
                hi, lo = split(x_ref[256 * c : 256 * c + 256, :].T)
                xt_ref[0, c], xt_ref[1, c] = hi, lo
            hi, lo = xt_ref[0, c], xt_ref[1, c]
            res = dot(hi, th, 1, 0) + dot(hi, tl, 1, 0) + dot(lo, th, 1, 0)
            for b in range(2):
                stage_ref[2 * half + b, pl.ds(c, 128, stride=16), :] = res[:, 128 * b : 128 * b + 128]
        for b in range(2 * half, 2 * half + 2):
            copy = pltpu.make_async_copy(stage_ref.at[b], out_ref.at[:, pl.ds(128 * b, 128)], sem.at[b])
            copy.start()
            copies.append(copy)
    for copy in copies:
        copy.wait()


def body(recording, source_channels):
    fwd_hi, fwd_lo = (jnp.asarray(t) for t in split_np(forward_table()))
    inv_hi, inv_lo = (jnp.asarray(t) for t in split_np(inverse_table()))
    dma = pltpu.SemaphoreType.DMA
    cross = pl.pallas_call(
        exchange_kernel,
        out_shape=jax.ShapeDtypeStruct((16 * 256, 128), F32),
        in_specs=[SMEM, ANY, ANY, ANY],
        out_specs=VMEM,
        scratch_shapes=[
            pltpu.VMEM((256, L), F32),
            pltpu.VMEM((256, L), BF),
            pltpu.VMEM((256, L), BF),
            pltpu.VMEM((512, 128), F32),
            pltpu.VMEM((512, 128), F32),
            pltpu.VMEM((2, NZ, 32, 128), F32),
            pltpu.VMEM((NJ, 8, 128), F32),
            pltpu.VMEM((2048, 128), F32),
            pltpu.VMEM((2, 64, 128), F32),
            pltpu.VMEM((3, 64, 128), F32),
            pltpu.VMEM((NJ, 2, 2, 32, 128), F32),
            pltpu.VMEM((2, 32, 16, 128), F32),
            pltpu.VMEM((64, 128, 128), BF),
            dma((3,)), dma, dma((2, NZ)), dma, dma, dma((3,)), dma((3,)), dma, dma, dma, dma((NJ, 2)),
        ],
        compiler_params=pltpu.CompilerParams(collective_id=0, has_side_effects=True),
        name="exchange",
    )(source_channels, recording.reshape(256, L), fwd_hi, fwd_lo)
    out = pl.pallas_call(
        output_kernel,
        out_shape=jax.ShapeDtypeStruct((128 * 16, LAGS), F32),
        in_specs=[VMEM] * 3,
        out_specs=ANY,
        scratch_shapes=[
            pltpu.VMEM((2, 16, 128, 256), BF),
            pltpu.VMEM((4, 2048, 128), F32),
            dma((4,)),
        ],
        name="correlate",
    )(cross, inv_hi, inv_lo)
    return out.reshape(128, 16, LAGS)


def solution(mesh):
    return jax.shard_map(
        body,
        mesh=mesh,
        in_specs=(P("half", "shard", None), P()),
        out_specs=P("half", "shard", None),
        check_vma=False,
    )
```

```python
import functools

import jax
import jax.numpy as jnp
import numpy as np
from jax import lax
from jax.experimental import pallas as pl
from jax.experimental.pallas import tpu as pltpu
from jax.sharding import PartitionSpec as P

F = 128
L = 1024
LAGS = 512
SEG = 32
water_level = 0.2
epsilon = 1e-05

NX, NZ = 4, 8
NJ = 64
ANY = pl.BlockSpec(memory_space=pl.ANY)
VMEM = pl.BlockSpec(memory_space=pltpu.VMEM)
SMEM = pl.BlockSpec(memory_space=pltpu.SMEM)
MESH = pl.DeviceIdType.MESH
BF = jnp.bfloat16
F32 = jnp.float32


def split_np(table):
    hi = table.astype(np.float32).astype(jnp.bfloat16)
    lo = (table - hi.astype(np.float64)).astype(np.float32).astype(jnp.bfloat16)
    return hi, lo


def forward_table():
    bins = np.arange(F) + 1
    times = np.arange(L)
    angle = 2.0 * np.pi * (bins[:, None] * times[None, :] % L) / L
    taper = 0.5 - 0.5 * np.cos(2.0 * np.pi * times / L)
    return np.concatenate((np.cos(angle) * taper, -np.sin(angle) * taper), axis=0)


def inverse_table():
    bins = np.arange(F) + 1
    shifts = np.arange(LAGS) - LAGS // 2
    angle = 2.0 * np.pi * (bins[:, None] * shifts[None, :] % L) / L
    return np.concatenate((np.cos(angle), -np.sin(angle)), axis=0) / np.sqrt(SEG * F)


def split(v):
    hi = v.astype(BF)
    return hi, (v - hi.astype(F32)).astype(BF)


def dot(a, b, ca, cb):
    return lax.dot_general(a, b, (((ca,), (cb,)), ((), ())), preferred_element_type=F32)


OFF_Z = (1, -1, 2, -2, 3, -3, 4)
FIRST = (
    ((1, 0), (-1, 0), (0, 1), (0, -1), (0, -2)),
    ((-1, 0), (2, 0), (1, 0), (0, 1), (0, -1)),
)
GATHER = (
    (0, 0, 0, None), (1, 0, 0, None), (0, 1, 0, ((1, 0), (0, -1), (0, 1))), (0, 0, 1, ()),
    (1, -1, 0, ((-1, 0), (0, -1))), (0, 0, -1, ()), (0, -1, 0, ((-1, 0), (0, 1), (0, -1))),
    (1, 0, 1, ((0, 1), (-1, 0))), (0, -1, 0, None), (0, 0, -1, None), (1, 1, 0, ((3, 0), (0, 1))), (1, 1, 0, None),
    (0, 0, 1, None), (1, 0, -1, ((1, 0),)), (0, 1, 0, None), (1, 2, 0, ((1, 0), (0, -2), (0, -1))), (1, 0, -1, None),
    (0, 0, 2, ()), (0, 2, 0, ((0, -1), (1, 0))), (0, 1, -1, ((0, -1),)), (1, -1, 0, None),
    (1, -2, 0, ((-1, 0), (0, -2), (0, -1))), (0, 1, 1, ((1, 0),)), (1, 0, 1, None), (0, -2, 0, ((-1, 0), (0, 1))),
    (1, -1, -1, ()), (1, -2, 0, None), (1, -1, 1, ()), (0, 0, 2, None), (0, -1, 1, ()), (0, -1, -1, ()),
    (1, 1, -1, ((0, -1),)), (0, -2, 0, None), (1, 0, 2, ()), (0, -1, 1, None), (1, 3, 0, ((0, 1),)),
    (1, 1, 1, ((1, 0),)), (0, 2, 0, None), (0, -1, -1, None), (1, 1, -1, None), (0, 1, -1, None), (1, -1, 1, None),
    (1, 2, -1, ()), (0, 1, 1, None), (0, 3, 0, ((0, 1),)), (0, 2, -1, ((1, 0), (0, -1))), (1, 4, 0, ((0, 1),)),
    (1, 0, 2, None), (0, 1, 2, ((3, 0),)), (0, -3, 0, ((0, 1), (-1, 0))), (1, 2, 2, ((2, 0),)), (1, 2, 0, None),
    (0, 2, 1, ()), (1, -1, -1, None), (0, -2, 1, ((0, 1),)), (1, 1, 1, None), (1, 1, 2, ()), (1, -3, 0, ((0, -1),)),
    (1, -3, 0, None), (1, 2, 1, ()), (1, -2, -1, ((-2, 0),)), (1, 3, 1, ((0, 1),)), (1, 4, 0, None),
    (1, -2, 2, ((1, 0), (0, -1))), (1, -2, 2, None), (0, -3, 0, None), (0, -2, 1, None), (0, 3, 0, None),
    (0, 2, -1, None), (1, -2, -1, None), (1, 4, 1, ((1, 0),)), (1, 3, 0, None), (0, 3, 1, ((0, 1),)), (1, 2, 1, None),
    (0, 3, -1, ((2, 0), (1, 0))), (0, 2, 2, ()), (1, 2, 2, None), (0, -3, 1, ((0, 1),)), (0, 4, 0, ((0, 1),)),
    (0, -2, 2, ((1, 0), (0, 1))), (1, 4, 2, ()), (1, -3, -1, ((-2, 0), (0, -1))), (1, -3, -1, None), (0, -2, 2, None),
    (1, -2, 1, ()), (1, -2, 1, None), (0, -3, 1, None), (0, 4, 2, ()), (0, 2, 2, None), (1, 3, 2, ()),
    (1, 4, 2, None), (1, -1, 2, ()), (1, -1, 2, None), (0, 4, 0, None), (1, 4, -1, ()), (0, 3, -1, None),
    (1, 4, -1, None), (1, 3, 1, None), (1, -3, 1, ()), (0, 4, 2, None), (0, -2, -1, ()), (0, -2, -1, None),
    (1, 4, 1, None), (0, 3, 2, ()), (0, 4, -1, ()), (0, 4, 1, ()), (0, -1, 2, ()), (0, -1, 2, None), (0, -3, 2, ()),
    (1, 1, 2, None), (1, -3, 2, ()), (0, -3, -1, ()), (1, -3, 2, None), (0, -3, -1, None), (1, 2, -1, None),
    (1, 3, -1, ()), (0, 2, 1, None), (1, 3, -1, None), (0, 1, 2, None), (0, -3, 2, None), (0, 3, 2, None),
    (0, 4, 1, None), (0, 4, -1, None), (1, 3, 2, None), (0, 3, 1, None), (1, -3, 1, None),
)


def whiten(rec_ref, hi_ref, lo_ref, out_ref):
    rec_hi, rec_lo = split(rec_ref[...])
    spec = dot(hi_ref[...], rec_hi, 1, 1) + dot(hi_ref[...], rec_lo, 1, 1) + dot(lo_ref[...], rec_hi, 1, 1)
    re, im = spec[:F], spec[F:]
    mag = jnp.sqrt(re * re + im * im)
    zeros = jnp.zeros((2, mag.shape[1]), F32)
    pad = jnp.concatenate((zeros, mag, zeros), axis=0)
    smooth = pad[0:F]
    for off in range(1, 5):
        smooth = smooth + pad[off : off + F]
    mean = jnp.sum(mag, axis=0, keepdims=True) * (1.0 / F)
    divisor = smooth / 5.0 + water_level * mean + epsilon
    for q, part in enumerate((re, im)):
        white = part / divisor
        for s_hi in range(2):
            out_ref[pl.ds(2 * q + s_hi, F, stride=4), :] = white[:, 128 * s_hi : 128 * (s_hi + 1)]


def swap(v, bit, lane):
    step = 1 << bit
    low = (lane & step) == 0
    v = list(v)
    for i in range(len(v)):
        if i & step:
            continue
        a, b = v[i], v[i + step]
        v[i] = jnp.where(low, a, pltpu.roll(b, step, 1))
        v[i + step] = jnp.where(low, pltpu.roll(a, 128 - step, 1), b)
    return v


def lanes():
    return lax.broadcasted_iota(jnp.int32, (16, 128), 1)


def receivers_first(ref, mid_ref, side):
    v = []
    for e in range(4):
        t = ref[pl.ds(e, F, stride=4), :].T
        v += [t[16 * i : 16 * i + 16] for i in range(8)]
    for bit in range(5):
        v = swap(v, bit, lanes())
    for i in range(32):
        mid_ref[side, i] = v[i]


def receivers_last(mid_ref, lhs_ref):
    lane = lanes()
    first = (lane & 16) == 0
    top = lane < 64
    low = (lane & 32) == 0
    for i in range(32):
        a, b = mid_ref[0, i], mid_ref[1, i]
        pair = (jnp.where(low, a, pltpu.roll(b, 32, 1)), jnp.where(low, pltpu.roll(a, 96, 1), b))
        for half in range(2):
            a = pair[half]
            b = jnp.where(first, pltpu.roll(a, 112, 1), -pltpu.roll(a, 16, 1))
            rows = []
            for r in (a, b):
                rows.append(jnp.where(top, r, 0.0))
                rows.append(jnp.where(top, 0.0, r))
            hi, lo = split(jnp.concatenate(rows, axis=0))
            lhs_ref[32 * half + i] = jnp.concatenate((hi, lo), axis=0)


def exchange_kernel(idx_ref, rec_hbm, hi_hbm, lo_hbm, x_ref, rec_ref, hi_ref, lo_ref, w_ref, wo_ref, z_ref, a_ref,
                    gm_ref, pick_ref, y_ref, g_ref, mid_ref, lhs_ref,
                    load, z_send, z_recv, a_send, a_recv, y_send, y_recv, wo_send, wo_recv, g_send, g_recv):
    h = lax.axis_index("half")
    s = lax.axis_index("shard")
    yh, u, k = s // NJ, (s % NJ) // 2, s % 2
    z, x = u // NX, u % NX
    j = k * 32 + u

    def device(zz, xx, kk):
        return (h, yh * NJ + (zz * NX + xx) * 2 + kk)

    def zat(d):
        return (z + d + NZ) % NZ

    def xat(d):
        return (x + d + NX) % NX

    def remote(src, dst, ssem, rsem, dev):
        return pltpu.make_async_remote_copy(
            src_ref=src, dst_ref=dst, send_sem=ssem, recv_sem=rsem, device_id=dev, device_id_type=MESH
        )

    plane = [(xat(d), kk) for d in (0, 1, -1, 2) for kk in (k, 1 - k)][1:]
    ring_y = [(h, (1 - yh) * NJ + s % NJ), (1 - h, s), (1 - h, (1 - yh) * NJ + s % NJ)]
    barrier = pltpu.get_barrier_semaphore()
    for dev in [device(zat(d), x, k) for d in OFF_Z] + [device(z, *p) for p in plane] + ring_y:
        pl.semaphore_signal(barrier, inc=1, device_id=dev, device_id_type=MESH)
    loads = [
        pltpu.make_async_copy(a, b, load.at[i])
        for i, (a, b) in enumerate(((rec_hbm, rec_ref), (hi_hbm, hi_ref), (lo_hbm, lo_ref)))
    ]
    for c in loads:
        c.start()
    for c in loads:
        c.wait()
    whiten(rec_ref, hi_ref, lo_ref, w_ref)
    pl.semaphore_wait(barrier, 17)

    def rows(kk, zz, n):
        return pl.ds(pl.multiple_of((kk * 32 + zz * NX) * 8, 8), n)

    for d in OFF_Z:
        for kk in range(2):
            remote(
                w_ref.at[rows(kk, zat(d), 32)], z_ref.at[kk, z], z_send, z_recv.at[kk, z], device(zat(d), x, k)
            ).start()
    wo = remote(w_ref, wo_ref, wo_send, wo_recv, ring_y[1])
    wo.start()
    for kk in range(2):
        z_ref[kk, z] = w_ref[rows(kk, z, 32), :]
    receivers_first(w_ref, mid_ref, 0)
    for d in (0,) + OFF_Z:
        zs = zat(d)
        if d:
            for kk in range(2):
                remote(z_ref.at[kk, zs], z_ref.at[kk, zs], z_send, z_recv.at[kk, zs], ring_y[0]).wait_recv()
        mine = k * 32 + zs * NX + x
        for xx, kk in plane:
            src = z_ref.at[kk, zs, pl.ds(pl.multiple_of(xx * 8, 8), 8)]
            remote(src, a_ref.at[mine], a_send, a_recv, device(z, xx, kk)).start()
        a_ref[mine] = z_ref[k, zs, pl.ds(pl.multiple_of(x * 8, 8), 8), :]
    some_a = remote(a_ref.at[pl.ds(0, 56)], a_ref.at[pl.ds(0, 56)], a_send, a_recv, ring_y[0])
    some_a.wait_recv()

    lane_c = lax.broadcasted_iota(jnp.int32, (8, 128), 1) & 15

    def pick(n, carry):
        q = idx_ref[n]
        p = q >> 4
        c = jnp.where((p >> 6) == yh, q & 15, 99)
        v = jnp.where(lane_c == c, a_ref[(p & 1) * 32 + ((p & 63) >> 1)], 0.0)
        gm_ref[pl.ds(n, 8, stride=256), :] = v
        return carry

    lax.fori_loop(0, 256, pick, 0, unroll=8)
    row = lax.broadcasted_iota(jnp.int32, (8, 128), 0)
    col = lax.broadcasted_iota(jnp.int32, (8, 128), 1)
    fold = jnp.where((col >> 4) == row, 1.0, 0.0).astype(BF)
    for e in range(8):
        v = gm_ref[256 * e : 256 * (e + 1), :]
        hi = v.astype(BF)
        rest = v - hi.astype(F32)
        mid = rest.astype(BF)
        lo = (rest - mid.astype(F32)).astype(BF)
        got = dot(fold, hi, 1, 1) + dot(fold, mid, 1, 1) + dot(fold, lo, 1, 1)
        pick_ref[0, 8 * e : 8 * (e + 1), :] = got[:, :128]
        pick_ref[1, 8 * e : 8 * (e + 1), :] = got[:, 128:]

    trades = [
        remote(pick_ref.at[h], y_ref.at[0], y_send.at[0], y_recv.at[0], ring_y[0]),
        remote(pick_ref.at[1 - h], y_ref.at[1], y_send.at[1], y_recv.at[1], ring_y[1]),
        remote(pick_ref.at[1 - h], y_ref.at[2], y_send.at[2], y_recv.at[2], ring_y[2]),
    ]
    for t in trades:
        t.start()
    wo.wait()
    receivers_first(wo_ref, mid_ref, 1)
    receivers_last(mid_ref, lhs_ref)
    for t in trades:
        t.wait()
    own = pick_ref[h] + y_ref[0]
    other = y_ref[1] + y_ref[2]
    for f2 in range(2):
        g_ref[j, f2, 0] = own[32 * f2 : 32 * f2 + 32]
        g_ref[j, f2, 1] = other[32 * f2 : 32 * f2 + 32]

    sign = 1 - 2 * k

    def source(dz, dx):
        return zat(-sign * dz) * NX + xat(-sign * dx)

    def pass_on(u2, f2, targets):
        blk = g_ref.at[k * 32 + u2, f2]
        devices = [device(zat(sign * dz), xat(sign * dx), k) for dz, dx in targets] + [device(z, x, 1 - k)]
        for dev in devices:
            remote(blk, blk, g_send, g_recv.at[k * 32 + u2, f2], dev).start()

    def arrived(kk, u2, f2):
        blk = g_ref.at[kk * 32 + u2, f2]
        remote(blk, blk, g_send, g_recv.at[kk * 32 + u2, f2], ring_y[0]).wait_recv()

    def cross(u2, f2):
        arrived(1 - k, u2, f2)
        g = u2 * 2 + f2
        src = jnp.concatenate((g_ref[u2, f2].reshape(64, 128), g_ref[32 + u2, f2].reshape(64, 128)), axis=0)
        hi, lo = split(src)
        res = dot(lhs_ref[g], jnp.concatenate((hi, lo), axis=1), 1, 0)
        res = res[:64, :128] + (res[:64, 128:] + res[64:, :128])
        for i in range(4):
            x_ref[pl.ds(64 * i + g, 16, stride=256), :] = res[16 * i : 16 * i + 16]

    for f2 in range(2):
        pass_on(u, f2, FIRST[f2])
    for f2, dz, dx, targets in GATHER:
        u2 = source(dz, dx)
        if targets is None:
            cross(u2, f2)
        else:
            arrived(k, u2, f2)
            pass_on(u2, f2, targets)
    most_g = g_ref.at[pl.ds(0, NJ - 1)]
    remote(most_g, most_g, g_send, a_recv, ring_y[0]).wait_send()
    some_a.wait_send()
    sent_z = w_ref.at[pl.ds(0, 448)]
    remote(sent_z, sent_z, z_send, a_recv, ring_y[0]).wait_send()


def output_kernel(x_ref, hi_ref, lo_ref, out_ref, xt_ref, stage_ref, sem):
    copies = []
    for half in range(2):
        th = hi_ref[:, 256 * half : 256 * half + 256]
        tl = lo_ref[:, 256 * half : 256 * half + 256]
        for c in range(16):
            if half == 0:
                hi, lo = split(x_ref[256 * c : 256 * c + 256, :].T)
                xt_ref[0, c], xt_ref[1, c] = hi, lo
            hi, lo = xt_ref[0, c], xt_ref[1, c]
            res = dot(hi, th, 1, 0) + dot(hi, tl, 1, 0) + dot(lo, th, 1, 0)
            for b in range(2):
                stage_ref[2 * half + b, pl.ds(c, 128, stride=16), :] = res[:, 128 * b : 128 * b + 128]
        for b in range(2 * half, 2 * half + 2):
            copy = pltpu.make_async_copy(stage_ref.at[b], out_ref.at[:, pl.ds(128 * b, 128)], sem.at[b])
            copy.start()
            copies.append(copy)
    for copy in copies:
        copy.wait()


def body(recording, source_channels):
    fwd_hi, fwd_lo = (jnp.asarray(t) for t in split_np(forward_table()))
    inv_hi, inv_lo = (jnp.asarray(t) for t in split_np(inverse_table()))
    dma = pltpu.SemaphoreType.DMA
    cross = pl.pallas_call(
        exchange_kernel,
        out_shape=jax.ShapeDtypeStruct((16 * 256, 128), F32),
        in_specs=[SMEM, ANY, ANY, ANY],
        out_specs=VMEM,
        scratch_shapes=[
            pltpu.VMEM((256, L), F32),
            pltpu.VMEM((256, L), BF),
            pltpu.VMEM((256, L), BF),
            pltpu.VMEM((512, 128), F32),
            pltpu.VMEM((512, 128), F32),
            pltpu.VMEM((2, NZ, 32, 128), F32),
            pltpu.VMEM((NJ, 8, 128), F32),
            pltpu.VMEM((2048, 128), F32),
            pltpu.VMEM((2, 64, 128), F32),
            pltpu.VMEM((3, 64, 128), F32),
            pltpu.VMEM((NJ, 2, 2, 32, 128), F32),
            pltpu.VMEM((2, 32, 16, 128), F32),
            pltpu.VMEM((64, 128, 128), BF),
            dma((3,)), dma, dma((2, NZ)), dma, dma, dma((3,)), dma((3,)), dma, dma, dma, dma((NJ, 2)),
        ],
        compiler_params=pltpu.CompilerParams(collective_id=0, has_side_effects=True),
        name="exchange",
    )(source_channels, recording.reshape(256, L), fwd_hi, fwd_lo)
    out = pl.pallas_call(
        output_kernel,
        out_shape=jax.ShapeDtypeStruct((128 * 16, LAGS), F32),
        in_specs=[VMEM] * 3,
        out_specs=ANY,
        scratch_shapes=[
            pltpu.VMEM((2, 16, 128, 256), BF),
            pltpu.VMEM((4, 2048, 128), F32),
            dma((4,)),
        ],
        name="correlate",
    )(cross, inv_hi, inv_lo)
    return out.reshape(128, 16, LAGS)


def solution(mesh):
    return jax.shard_map(
        body,
        mesh=mesh,
        in_specs=(P("half", "shard", None), P()),
        out_specs=P("half", "shard", None),
        check_vma=False,
    )
```

```python
import functools

import jax
import jax.numpy as jnp
import numpy as np
from jax import lax
from jax.experimental import pallas as pl
from jax.experimental.pallas import tpu as pltpu
from jax.sharding import PartitionSpec as P

F = 128
L = 1024
LAGS = 512
SEG = 32
water_level = 0.2
epsilon = 1e-05

NX, NZ = 4, 8
NJ = 64
ANY = pl.BlockSpec(memory_space=pl.ANY)
VMEM = pl.BlockSpec(memory_space=pltpu.VMEM)
HBM = pl.BlockSpec(memory_space=pltpu.HBM)
MESH = pl.DeviceIdType.MESH
BF = jnp.bfloat16
F32 = jnp.float32


def split_np(table):
    hi = table.astype(np.float32).astype(jnp.bfloat16)
    lo = (table - hi.astype(np.float64)).astype(np.float32).astype(jnp.bfloat16)
    return hi, lo


def forward_table():
    bins = np.arange(F) + 1
    times = np.arange(L)
    angle = 2.0 * np.pi * (bins[:, None] * times[None, :] % L) / L
    taper = 0.5 - 0.5 * np.cos(2.0 * np.pi * times / L)
    return np.concatenate((np.cos(angle) * taper, -np.sin(angle) * taper), axis=0)


def inverse_table():
    bins = np.arange(F) + 1
    shifts = np.arange(LAGS) - LAGS // 2
    angle = 2.0 * np.pi * (bins[:, None] * shifts[None, :] % L) / L
    table = np.stack((np.cos(angle), -np.sin(angle)), axis=1) / np.sqrt(SEG * F)
    return table.reshape(2, 32, 2, 2, LAGS).transpose(1, 2, 0, 3, 4).reshape(2 * F, LAGS)


def split(v):
    hi = v.astype(BF)
    return hi, (v - hi.astype(F32)).astype(BF)


def dot(a, b, ca, cb):
    return lax.dot_general(a, b, (((ca,), (cb,)), ((), ())), preferred_element_type=F32)


OFF_Z = (1, -1, 2, -2, 3, -3, 4)
FIRST = (
    ((1, 0), (-1, 0), (0, 1), (0, -1), (0, -2)),
    ((-1, 0), (2, 0), (1, 0), (0, 1), (0, -1)),
)
GATHER = (
    (1, 0, 0, None), (0, 1, 0, ((1, 0), (0, -1), (0, 1))), (0, 0, 1, ()), (1, -1, 0, ((-1, 0), (0, -1))),
    (0, 0, -1, ()), (0, -1, 0, ((-1, 0), (0, 1), (0, -1))), (1, 0, 1, ((0, 1), (-1, 0))), (1, 1, 0, ((3, 0), (0, 1))),
    (1, 0, -1, ((1, 0),)), (0, 1, 0, None), (1, 2, 0, ((1, 0), (0, -2), (0, -1))), (1, 0, -1, None), (0, 0, 2, ()),
    (0, 2, 0, ((0, -1), (1, 0))), (0, 1, -1, ((0, -1),)), (1, -1, 0, None), (1, -2, 0, ((-1, 0), (0, -2), (0, -1))),
    (0, 1, 1, ((1, 0),)), (1, 0, 1, None), (0, -2, 0, ((-1, 0), (0, 1))), (1, -1, -1, ()), (1, -1, 1, ()),
    (0, -1, 1, ()), (0, -1, -1, ()), (1, 1, -1, ((0, -1),)), (0, -2, 0, None), (1, 0, 2, ()), (1, 3, 0, ((0, 1),)),
    (1, 1, 1, ((1, 0),)), (0, 1, -1, None), (1, -1, 1, None), (1, 2, -1, ()), (0, 3, 0, ((0, 1),)),
    (0, 2, -1, ((1, 0), (0, -1))), (1, 4, 0, ((0, 1),)), (1, 0, 2, None), (0, 1, 2, ((3, 0),)),
    (0, -3, 0, ((0, 1), (-1, 0))), (1, 2, 2, ((2, 0),)), (1, 2, 0, None), (0, 2, 1, ()), (1, -1, -1, None),
    (0, -2, 1, ((0, 1),)), (1, 1, 1, None), (1, 1, 2, ()), (1, -3, 0, ((0, -1),)), (1, 2, 1, ()),
    (1, -2, -1, ((-2, 0),)), (1, 3, 1, ((0, 1),)), (1, -2, 2, ((1, 0), (0, -1))), (0, -3, 0, None),
    (1, 4, 1, ((1, 0),)), (1, 3, 0, None), (0, 3, 1, ((0, 1),)), (0, 3, -1, ((2, 0), (1, 0))), (0, 2, 2, ()),
    (0, -3, 1, ((0, 1),)), (0, 4, 0, ((0, 1),)), (0, -2, 2, ((1, 0), (0, 1))), (1, 4, 2, ()),
    (1, -3, -1, ((-2, 0), (0, -1))), (0, -2, 2, None), (1, -2, 1, ()), (1, -2, 1, None), (0, 4, 2, ()),
    (0, 2, 2, None), (1, 3, 2, ()), (1, -1, 2, ()), (0, 4, 0, None), (1, 4, -1, ()), (1, -3, 1, ()), (0, 4, 2, None),
    (0, -2, -1, ()), (0, -2, -1, None), (0, 3, 2, ()), (0, 4, -1, ()), (0, 4, 1, ()), (0, -1, 2, ()),
    (0, -1, 2, None), (0, -3, 2, ()), (1, -3, 2, ()), (0, -3, -1, ()), (0, -3, -1, None), (1, 2, -1, None),
    (1, 3, -1, ()), (0, 2, 1, None), (1, 3, -1, None), (0, 1, 2, None), (0, -3, 2, None), (0, 4, 1, None),
    (0, 4, -1, None), (1, 3, 2, None), (0, 3, 1, None), (1, -3, 1, None),
)


def whiten(rec_ref, hi_ref, lo_ref, out_ref):
    rec_hi, rec_lo = split(rec_ref[...])
    spec = dot(hi_ref[...], rec_hi, 1, 1) + dot(hi_ref[...], rec_lo, 1, 1) + dot(lo_ref[...], rec_hi, 1, 1)
    re, im = spec[:F], spec[F:]
    mag = jnp.sqrt(re * re + im * im)
    zeros = jnp.zeros((2, mag.shape[1]), F32)
    pad = jnp.concatenate((zeros, mag, zeros), axis=0)
    smooth = pad[0:F]
    for off in range(1, 5):
        smooth = smooth + pad[off : off + F]
    mean = jnp.sum(mag, axis=0, keepdims=True) * (1.0 / F)
    divisor = smooth / 5.0 + water_level * mean + epsilon
    for q, part in enumerate((re, im)):
        white = part / divisor
        for s_hi in range(2):
            out_ref[pl.ds(2 * q + s_hi, F, stride=4), :] = white[:, 128 * s_hi : 128 * (s_hi + 1)]


def swap(v, bit, lane):
    step = 1 << bit
    low = (lane & step) == 0
    v = list(v)
    for i in range(len(v)):
        if i & step:
            continue
        a, b = v[i], v[i + step]
        v[i] = jnp.where(low, a, pltpu.roll(b, step, 1))
        v[i + step] = jnp.where(low, pltpu.roll(a, 128 - step, 1), b)
    return v


def lanes():
    return lax.broadcasted_iota(jnp.int32, (16, 128), 1)


def receivers_first(ref, mid_ref, side):
    v = []
    for e in range(4):
        t = ref[pl.ds(e, F, stride=4), :].T
        v += [t[16 * i : 16 * i + 16] for i in range(8)]
    for bit in range(5):
        v = swap(v, bit, lanes())
    for i in range(32):
        mid_ref[side, i] = v[i]


def receivers_last(mid_ref, lhs_ref):
    lane = lanes()
    first = (lane & 16) == 0
    low = (lane & 32) == 0
    row8 = lax.broadcasted_iota(jnp.int32, (8, 128), 0)
    lane8 = lax.broadcasted_iota(jnp.int32, (8, 128), 1)
    imag = (row8 & 1) == 1
    same = ((row8 >> 1) & 1) == (lane8 >> 6)
    keep = [same & ((row8 >> 2) == f2) for f2 in range(2)]
    for i in range(32):
        a, b = mid_ref[0, i], mid_ref[1, i]
        pair = (jnp.where(low, a, pltpu.roll(b, 32, 1)), jnp.where(low, pltpu.roll(a, 96, 1), b))
        for half in range(2):
            g = 32 * half + i
            u, f2 = g // 2, g % 2
            re = pair[half]
            im = jnp.where(first, pltpu.roll(re, 112, 1), -pltpu.roll(re, 16, 1))
            rows = []
            for c in range(16):
                v = jnp.where(
                    imag, jnp.broadcast_to(im[c : c + 1], (8, 128)), jnp.broadcast_to(re[c : c + 1], (8, 128))
                )
                rows.append(jnp.where(keep[f2], v, 0.0))
            hi, lo = split(jnp.concatenate(rows, axis=0))
            lhs_ref[u, 0:128, 128 * f2 : 128 * f2 + 128] = hi
            lhs_ref[u, 128:256, 128 * f2 : 128 * f2 + 128] = lo


def exchange_kernel(idx_hbm, rec_hbm, hi_hbm, lo_hbm, x_ref, idx_ref, rec_ref, hi_ref, lo_ref, w_ref, wo_ref, z_ref, a_ref,
                    gm_ref, pick_ref, y_ref, g_ref, mid_ref, lhs_ref,
                    load, z_send, z_recv, a_send, a_recv, y_send, y_recv, wo_send, wo_recv, g_send, g_recv):
    h = lax.axis_index("half")
    s = lax.axis_index("shard")
    yh, u, k = s // NJ, (s % NJ) // 2, s % 2
    z, x = u // NX, u % NX
    j = k * 32 + u

    def device(zz, xx, kk):
        return (h, yh * NJ + (zz * NX + xx) * 2 + kk)

    def zat(d):
        return (z + d + NZ) % NZ

    def xat(d):
        return (x + d + NX) % NX

    def remote(src, dst, ssem, rsem, dev):
        return pltpu.make_async_remote_copy(
            src_ref=src, dst_ref=dst, send_sem=ssem, recv_sem=rsem, device_id=dev, device_id_type=MESH
        )

    plane = [(xat(d), kk) for d in (0, 1, -1, 2) for kk in (k, 1 - k)][1:]
    ring_y = [(h, (1 - yh) * NJ + s % NJ), (1 - h, s), (1 - h, (1 - yh) * NJ + s % NJ)]
    barrier = pltpu.get_barrier_semaphore()
    for dev in [device(zat(d), x, k) for d in OFF_Z] + [device(z, *p) for p in plane] + ring_y:
        pl.semaphore_signal(barrier, inc=1, device_id=dev, device_id_type=MESH)
    loads = [
        pltpu.make_async_copy(a, b, load.at[i])
        for i, (a, b) in enumerate(((rec_hbm, rec_ref), (hi_hbm, hi_ref), (lo_hbm, lo_ref), (idx_hbm, idx_ref)))
    ]
    for c in loads:
        c.start()
    for c in loads:
        c.wait()
    whiten(rec_ref, hi_ref, lo_ref, w_ref)
    pl.semaphore_wait(barrier, 17)

    def rows(kk, zz, n):
        return pl.ds(pl.multiple_of((kk * 32 + zz * NX) * 8, 8), n)

    for d in OFF_Z:
        for kk in range(2):
            remote(
                w_ref.at[rows(kk, zat(d), 32)], z_ref.at[kk, z], z_send, z_recv.at[kk, z], device(zat(d), x, k)
            ).start()
    wo = remote(w_ref, wo_ref, wo_send, wo_recv, ring_y[1])
    wo.start()
    for kk in range(2):
        z_ref[kk, z] = w_ref[rows(kk, z, 32), :]
    receivers_first(w_ref, mid_ref, 0)
    for d in (0,) + OFF_Z:
        zs = zat(d)
        if d:
            for kk in range(2):
                remote(z_ref.at[kk, zs], z_ref.at[kk, zs], z_send, z_recv.at[kk, zs], ring_y[0]).wait_recv()
        mine = k * 32 + zs * NX + x
        for xx, kk in plane:
            src = z_ref.at[kk, zs, pl.ds(pl.multiple_of(xx * 8, 8), 8)]
            remote(src, a_ref.at[mine], a_send, a_recv, device(z, xx, kk)).start()
        a_ref[mine] = z_ref[k, zs, pl.ds(pl.multiple_of(x * 8, 8), 8), :]
    wo.wait()
    receivers_first(wo_ref, mid_ref, 1)
    receivers_last(mid_ref, lhs_ref)
    some_a = remote(a_ref.at[pl.ds(0, 56)], a_ref.at[pl.ds(0, 56)], a_send, a_recv, ring_y[0])
    some_a.wait_recv()

    lane_c = lax.broadcasted_iota(jnp.int32, (8, 128), 1) & 15

    row = lax.broadcasted_iota(jnp.int32, (8, 128), 0)
    fold = jnp.where((lax.broadcasted_iota(jnp.int32, (8, 128), 1) >> 4) == row, 1.0, 0.0).astype(BF)
    trades = [
        remote(pick_ref.at[1], y_ref.at[0], y_send.at[0], y_recv.at[0], ring_y[0]),
        remote(pick_ref.at[0], y_ref.at[1], y_send.at[1], y_recv.at[1], ring_y[1]),
        remote(pick_ref.at[0], y_ref.at[2], y_send.at[2], y_recv.at[2], ring_y[2]),
    ]
    for own in range(2):
        base = (h if own else 1 - h) * 128

        def pick(n, carry):
            q = idx_ref[base + n]
            p = q >> 4
            c = jnp.where((p >> 6) == yh, q & 15, 99)
            v = jnp.where(lane_c == c, a_ref[(p & 1) * 32 + ((p & 63) >> 1)], 0.0)
            gm_ref[own, pl.ds(n, 8, stride=128), :] = v
            return carry

        lax.fori_loop(0, 128, pick, 0, unroll=16)
        for e in range(8):
            v = gm_ref[own, 128 * e : 128 * (e + 1), :]
            hi = v.astype(BF)
            rest = v - hi.astype(F32)
            mid = rest.astype(BF)
            lo = (rest - mid.astype(F32)).astype(BF)
            pick_ref[own, 8 * e : 8 * (e + 1), :] = dot(fold, hi, 1, 1) + dot(fold, mid, 1, 1) + dot(fold, lo, 1, 1)
        if own:
            trades[0].start()
        else:
            trades[2].start()
            trades[1].start()
    for t in trades:
        t.wait()
    own = pick_ref[1] + y_ref[0]
    other = y_ref[1] + y_ref[2]
    for f2 in range(2):
        g_ref[j, f2, 0] = own[32 * f2 : 32 * f2 + 32]
        g_ref[j, f2, 1] = other[32 * f2 : 32 * f2 + 32]

    sign = 1 - 2 * k

    def source(dz, dx):
        return zat(-sign * dz) * NX + xat(-sign * dx)

    def pass_on(u2, f2, targets):
        blk = g_ref.at[k * 32 + u2, f2]
        devices = [device(zat(sign * dz), xat(sign * dx), k) for dz, dx in targets] + [device(z, x, 1 - k)]
        for dev in devices:
            remote(blk, blk, g_send, g_recv.at[k * 32 + u2, f2], dev).start()

    def arrived(kk, u2, f2):
        blk = g_ref.at[kk * 32 + u2, f2]
        remote(blk, blk, g_send, g_recv.at[kk * 32 + u2, f2], ring_y[0]).wait_recv()

    low_n = [(lax.broadcasted_iota(jnp.int32, (8, 128), 1) & (1 << bit)) == 0 for bit in range(4)]

    def cross(u2):
        blocks = []
        for f2 in range(2):
            arrived(1 - k, u2, f2)
            blocks += [g_ref[u2, f2].reshape(64, 128), g_ref[32 + u2, f2].reshape(64, 128)]
        hi, lo = split(jnp.concatenate(blocks, axis=0))
        res = dot(lhs_ref[u2], jnp.concatenate((hi, lo), axis=1), 1, 0)
        res = res[:128, :128] + (res[:128, 128:] + res[128:, :128])
        v = [res[8 * c : 8 * c + 8] for c in range(16)]
        for bit in range(4):
            step = 1 << bit
            for i in range(16):
                if i & step:
                    continue
                a, b = v[i], v[i + step]
                v[i] = jnp.where(low_n[bit], a, pltpu.roll(b, step, 1))
                v[i + step] = jnp.where(low_n[bit], pltpu.roll(a, 128 - step, 1), b)
        at = pl.ds(pl.multiple_of(8 * u2, 8), 8)
        for i in range(16):
            x_ref[i, at, :] = v[i]

    for f2 in range(2):
        pass_on(u, f2, FIRST[f2])
    for f2, dz, dx, targets in GATHER:
        u2 = source(dz, dx)
        if targets is None:
            cross(u2)
        else:
            arrived(k, u2, f2)
            pass_on(u2, f2, targets)
    most_g = g_ref.at[pl.ds(0, NJ - 1)]
    remote(most_g, most_g, g_send, a_recv, ring_y[0]).wait_send()
    some_a.wait_send()
    sent_z = w_ref.at[pl.ds(0, 448)]
    remote(sent_z, sent_z, z_send, a_recv, ring_y[0]).wait_send()


def output_kernel(x_ref, hi_hbm, lo_hbm, out_ref, hi_ref, lo_ref, stage_ref, load, sem):
    loads = [
        pltpu.make_async_copy(hi_hbm, hi_ref, load.at[0]),
        pltpu.make_async_copy(lo_hbm, lo_ref, load.at[1]),
    ]
    for c in loads:
        c.start()
    copies = []
    for m in range(0, 16, 2):
        parts = [split(x_ref[i].T) for i in (m, m + 1)]
        hi = jnp.concatenate([p[0] for p in parts], axis=0)
        lo = jnp.concatenate([p[1] for p in parts], axis=0)
        if m == 0:
            for c in loads:
                c.wait()
        both = dot(jnp.concatenate((hi, lo), axis=0), hi_ref[...], 1, 0)
        res = both[:256] + (both[256:] + dot(hi, lo_ref[...], 1, 0))
        for i in range(2):
            stage_ref[m + i] = res[128 * i : 128 * i + 128].reshape(8, 16, LAGS)
            copy = pltpu.make_async_copy(stage_ref.at[m + i], out_ref.at[:, m + i], sem.at[m + i])
            copy.start()
            copies.append(copy)
    for copy in copies:
        copy.wait()


def body(recording, source_channels):
    fwd_hi, fwd_lo = (jnp.asarray(t) for t in split_np(forward_table()))
    inv_hi, inv_lo = (jnp.asarray(t) for t in split_np(inverse_table()))
    dma = pltpu.SemaphoreType.DMA
    cross = pl.pallas_call(
        exchange_kernel,
        out_shape=pltpu.VMEM((16, 256, 128), F32),
        in_specs=[HBM] * 4,
        out_specs=VMEM,
        scratch_shapes=[
            pltpu.SMEM((256,), jnp.int32),
            pltpu.VMEM((256, L), F32),
            pltpu.VMEM((256, L), BF),
            pltpu.VMEM((256, L), BF),
            pltpu.VMEM((512, 128), F32),
            pltpu.VMEM((512, 128), F32),
            pltpu.VMEM((2, NZ, 32, 128), F32),
            pltpu.VMEM((NJ, 8, 128), F32),
            pltpu.VMEM((2, 1024, 128), F32),
            pltpu.VMEM((2, 64, 128), F32),
            pltpu.VMEM((3, 64, 128), F32),
            pltpu.VMEM((NJ, 2, 2, 32, 128), F32),
            pltpu.VMEM((2, 32, 16, 128), F32),
            pltpu.VMEM((32, 256, 256), BF),
            dma((4,)), dma, dma((2, NZ)), dma, dma, dma((3,)), dma((3,)), dma, dma, dma, dma((NJ, 2)),
        ],
        compiler_params=pltpu.CompilerParams(collective_id=0, has_side_effects=True),
        name="exchange",
    )(source_channels, recording.reshape(256, L), fwd_hi, fwd_lo)
    out = pl.pallas_call(
        output_kernel,
        out_shape=jax.ShapeDtypeStruct((8, 16, 16, LAGS), F32),
        in_specs=[VMEM, ANY, ANY],
        out_specs=ANY,
        scratch_shapes=[
            pltpu.VMEM((256, LAGS), BF),
            pltpu.VMEM((256, LAGS), BF),
            pltpu.VMEM((16, 8, 16, LAGS), F32),
            dma((2,)),
            dma((16,)),
        ],
        compiler_params=pltpu.CompilerParams(vmem_limit_bytes=24 << 20),
        name="correlate",
    )(cross, inv_hi, inv_lo)
    return out.reshape(128, 16, LAGS)


def solution(mesh):
    return jax.shard_map(
        body,
        mesh=mesh,
        in_specs=(P("half", "shard", None), P()),
        out_specs=P("half", "shard", None),
        check_vma=False,
    )
```

```python
import functools

import jax
import jax.numpy as jnp
import numpy as np
from jax import lax
from jax.experimental import pallas as pl
from jax.experimental.pallas import tpu as pltpu
from jax.sharding import PartitionSpec as P

F = 128
L = 1024
LAGS = 512
SEG = 32
water_level = 0.2
epsilon = 1e-05

NX, NZ = 4, 8
NJ = 64
ANY = pl.BlockSpec(memory_space=pl.ANY)
VMEM = pl.BlockSpec(memory_space=pltpu.VMEM)
HBM = pl.BlockSpec(memory_space=pltpu.HBM)
MESH = pl.DeviceIdType.MESH
BF = jnp.bfloat16
F32 = jnp.float32


def split_np(table):
    hi = table.astype(np.float32).astype(jnp.bfloat16)
    lo = (table - hi.astype(np.float64)).astype(np.float32).astype(jnp.bfloat16)
    return hi, lo


def forward_table():
    bins = np.arange(F) + 1
    times = np.arange(L)
    angle = 2.0 * np.pi * (bins[:, None] * times[None, :] % L) / L
    taper = 0.5 - 0.5 * np.cos(2.0 * np.pi * times / L)
    return np.concatenate((np.cos(angle) * taper, -np.sin(angle) * taper), axis=0)


def inverse_table():
    bins = np.arange(F) + 1
    shifts = np.arange(LAGS) - LAGS // 2
    angle = 2.0 * np.pi * (bins[:, None] * shifts[None, :] % L) / L
    table = np.stack((np.cos(angle), -np.sin(angle)), axis=1) / np.sqrt(SEG * F)
    return table.reshape(2, 32, 2, 2, LAGS).transpose(1, 2, 0, 3, 4).reshape(2 * F, LAGS)


def split(v):
    hi = v.astype(BF)
    return hi, (v - hi.astype(F32)).astype(BF)


def dot(a, b, ca, cb):
    return lax.dot_general(a, b, (((ca,), (cb,)), ((), ())), preferred_element_type=F32)


OFF_Z = (1, -1, 2, -2, 3, -3, 4)
FIRST = (
    ((1, 0), (-1, 0), (0, 1), (0, -1), (0, -2)),
    ((-1, 0), (2, 0), (1, 0), (0, 1), (0, -1)),
)
GATHER = (
    (1, 0, 0, None), (0, 1, 0, ((1, 0), (0, -1), (0, 1))), (0, 0, 1, ()), (1, -1, 0, ((-1, 0), (0, -1))),
    (0, 0, -1, ()), (0, -1, 0, ((-1, 0), (0, 1), (0, -1))), (1, 0, 1, ((0, 1), (-1, 0))), (1, 1, 0, ((3, 0), (0, 1))),
    (1, 0, -1, ((1, 0),)), (0, 1, 0, None), (1, 2, 0, ((1, 0), (0, -2), (0, -1))), (1, 0, -1, None), (0, 0, 2, ()),
    (0, 2, 0, ((0, -1), (1, 0))), (0, 1, -1, ((0, -1),)), (1, -1, 0, None), (1, -2, 0, ((-1, 0), (0, -2), (0, -1))),
    (0, 1, 1, ((1, 0),)), (1, 0, 1, None), (0, -2, 0, ((-1, 0), (0, 1))), (1, -1, -1, ()), (1, -1, 1, ()),
    (0, -1, 1, ()), (0, -1, -1, ()), (1, 1, -1, ((0, -1),)), (0, -2, 0, None), (1, 0, 2, ()), (1, 3, 0, ((0, 1),)),
    (1, 1, 1, ((1, 0),)), (0, 1, -1, None), (1, -1, 1, None), (1, 2, -1, ()), (0, 3, 0, ((0, 1),)),
    (0, 2, -1, ((1, 0), (0, -1))), (1, 4, 0, ((0, 1),)), (1, 0, 2, None), (0, 1, 2, ((3, 0),)),
    (0, -3, 0, ((0, 1), (-1, 0))), (1, 2, 2, ((2, 0),)), (1, 2, 0, None), (0, 2, 1, ()), (1, -1, -1, None),
    (0, -2, 1, ((0, 1),)), (1, 1, 1, None), (1, 1, 2, ()), (1, -3, 0, ((0, -1),)), (1, 2, 1, ()),
    (1, -2, -1, ((-2, 0),)), (1, 3, 1, ((0, 1),)), (1, -2, 2, ((1, 0), (0, -1))), (0, -3, 0, None),
    (1, 4, 1, ((1, 0),)), (1, 3, 0, None), (0, 3, 1, ((0, 1),)), (0, 3, -1, ((2, 0), (1, 0))), (0, 2, 2, ()),
    (0, -3, 1, ((0, 1),)), (0, 4, 0, ((0, 1),)), (0, -2, 2, ((1, 0), (0, 1))), (1, 4, 2, ()),
    (1, -3, -1, ((-2, 0), (0, -1))), (0, -2, 2, None), (1, -2, 1, ()), (1, -2, 1, None), (0, 4, 2, ()),
    (0, 2, 2, None), (1, 3, 2, ()), (1, -1, 2, ()), (0, 4, 0, None), (1, 4, -1, ()), (1, -3, 1, ()), (0, 4, 2, None),
    (0, -2, -1, ()), (0, -2, -1, None), (0, 3, 2, ()), (0, 4, -1, ()), (0, 4, 1, ()), (0, -1, 2, ()),
    (0, -1, 2, None), (0, -3, 2, ()), (1, -3, 2, ()), (0, -3, -1, ()), (0, -3, -1, None), (1, 2, -1, None),
    (1, 3, -1, ()), (0, 2, 1, None), (1, 3, -1, None), (0, 1, 2, None), (0, -3, 2, None), (0, 4, 1, None),
    (0, 4, -1, None), (1, 3, 2, None), (0, 3, 1, None), (1, -3, 1, None),
)


def whiten(rec_ref, hi_ref, lo_ref, out_ref):
    rec_hi, rec_lo = split(rec_ref[...])
    spec = dot(hi_ref[...], rec_hi, 1, 1) + dot(hi_ref[...], rec_lo, 1, 1) + dot(lo_ref[...], rec_hi, 1, 1)
    re, im = spec[:F], spec[F:]
    mag = jnp.sqrt(re * re + im * im)
    zeros = jnp.zeros((2, mag.shape[1]), F32)
    pad = jnp.concatenate((zeros, mag, zeros), axis=0)
    smooth = pad[0:F]
    for off in range(1, 5):
        smooth = smooth + pad[off : off + F]
    mean = jnp.sum(mag, axis=0, keepdims=True) * (1.0 / F)
    divisor = smooth / 5.0 + water_level * mean + epsilon
    for q, part in enumerate((re, im)):
        white = part / divisor
        for s_hi in range(2):
            out_ref[pl.ds(2 * q + s_hi, F, stride=4), :] = white[:, 128 * s_hi : 128 * (s_hi + 1)]


def swap(v, bit, lane):
    step = 1 << bit
    low = (lane & step) == 0
    v = list(v)
    for i in range(len(v)):
        if i & step:
            continue
        a, b = v[i], v[i + step]
        v[i] = jnp.where(low, a, pltpu.roll(b, step, 1))
        v[i + step] = jnp.where(low, pltpu.roll(a, 128 - step, 1), b)
    return v


def lanes():
    return lax.broadcasted_iota(jnp.int32, (16, 128), 1)


def receivers_first(ref, mid_ref, side):
    v = []
    for e in range(4):
        t = ref[pl.ds(e, F, stride=4), :].T
        v += [t[16 * i : 16 * i + 16] for i in range(8)]
    for bit in range(5):
        v = swap(v, bit, lanes())
    for i in range(32):
        mid_ref[side, i] = v[i]


def receivers_last(mid_ref, lhs_ref):
    lane = lanes()
    first = (lane & 16) == 0
    low = (lane & 32) == 0
    row8 = lax.broadcasted_iota(jnp.int32, (8, 128), 0)
    lane8 = lax.broadcasted_iota(jnp.int32, (8, 128), 1)
    imag = (row8 & 1) == 1
    same = ((row8 >> 1) & 1) == (lane8 >> 6)
    keep = [same & ((row8 >> 2) == f2) for f2 in range(2)]
    for i in range(32):
        a, b = mid_ref[0, i], mid_ref[1, i]
        pair = (jnp.where(low, a, pltpu.roll(b, 32, 1)), jnp.where(low, pltpu.roll(a, 96, 1), b))
        for half in range(2):
            g = 32 * half + i
            u, f2 = g // 2, g % 2
            re = pair[half]
            im = jnp.where(first, pltpu.roll(re, 112, 1), -pltpu.roll(re, 16, 1))
            rows = []
            for c in range(16):
                v = jnp.where(
                    imag, jnp.broadcast_to(im[c : c + 1], (8, 128)), jnp.broadcast_to(re[c : c + 1], (8, 128))
                )
                rows.append(jnp.where(keep[f2], v, 0.0))
            hi, lo = split(jnp.concatenate(rows, axis=0))
            lhs_ref[u, 0:128, 128 * f2 : 128 * f2 + 128] = hi
            lhs_ref[u, 128:256, 128 * f2 : 128 * f2 + 128] = lo


def exchange_kernel(idx_hbm, rec_hbm, hi_hbm, lo_hbm, x_ref, idx_ref, rec_ref, hi_ref, lo_ref, w_ref, wo_ref, z_ref, a_ref,
                    gm_ref, pick_ref, y_ref, g_ref, mid_ref, lhs_ref,
                    load, z_send, z_recv, a_send, a_recv, y_send, y_recv, wo_send, wo_recv, g_send, g_recv):
    h = lax.axis_index("half")
    s = lax.axis_index("shard")
    yh, u, k = s // NJ, (s % NJ) // 2, s % 2
    z, x = u // NX, u % NX
    j = k * 32 + u

    def device(zz, xx, kk):
        return (h, yh * NJ + (zz * NX + xx) * 2 + kk)

    def zat(d):
        return (z + d + NZ) % NZ

    def xat(d):
        return (x + d + NX) % NX

    def remote(src, dst, ssem, rsem, dev):
        return pltpu.make_async_remote_copy(
            src_ref=src, dst_ref=dst, send_sem=ssem, recv_sem=rsem, device_id=dev, device_id_type=MESH
        )

    plane = [(xat(d), kk) for d in (0, 1, -1, 2) for kk in (k, 1 - k)][1:]
    ring_y = [(h, (1 - yh) * NJ + s % NJ), (1 - h, s), (1 - h, (1 - yh) * NJ + s % NJ)]
    barrier = pltpu.get_barrier_semaphore()
    for dev in [device(zat(d), x, k) for d in OFF_Z] + [device(z, *p) for p in plane] + ring_y:
        pl.semaphore_signal(barrier, inc=1, device_id=dev, device_id_type=MESH)
    loads = [
        pltpu.make_async_copy(a, b, load.at[i])
        for i, (a, b) in enumerate(((rec_hbm, rec_ref), (hi_hbm, hi_ref), (lo_hbm, lo_ref), (idx_hbm, idx_ref)))
    ]
    for c in loads:
        c.start()
    for c in loads:
        c.wait()
    whiten(rec_ref, hi_ref, lo_ref, w_ref)
    pl.semaphore_wait(barrier, 17)

    def rows(kk, zz, n):
        return pl.ds(pl.multiple_of((kk * 32 + zz * NX) * 8, 8), n)

    for d in OFF_Z:
        for kk in range(2):
            remote(
                w_ref.at[rows(kk, zat(d), 32)], z_ref.at[kk, z], z_send, z_recv.at[kk, z], device(zat(d), x, k)
            ).start()
    wo = remote(w_ref, wo_ref, wo_send, wo_recv, ring_y[1])
    wo.start()
    for kk in range(2):
        z_ref[kk, z] = w_ref[rows(kk, z, 32), :]
    receivers_first(w_ref, mid_ref, 0)
    for d in (0,) + OFF_Z:
        zs = zat(d)
        if d:
            for kk in range(2):
                remote(z_ref.at[kk, zs], z_ref.at[kk, zs], z_send, z_recv.at[kk, zs], ring_y[0]).wait_recv()
        mine = k * 32 + zs * NX + x
        for xx, kk in plane:
            src = z_ref.at[kk, zs, pl.ds(pl.multiple_of(xx * 8, 8), 8)]
            remote(src, a_ref.at[mine], a_send, a_recv, device(z, xx, kk)).start()
        a_ref[mine] = z_ref[k, zs, pl.ds(pl.multiple_of(x * 8, 8), 8), :]
    wo.wait()
    receivers_first(wo_ref, mid_ref, 1)
    receivers_last(mid_ref, lhs_ref)
    some_a = remote(a_ref.at[pl.ds(0, 56)], a_ref.at[pl.ds(0, 56)], a_send, a_recv, ring_y[0])
    some_a.wait_recv()

    lane_c = lax.broadcasted_iota(jnp.int32, (8, 128), 1) & 15

    row = lax.broadcasted_iota(jnp.int32, (8, 128), 0)
    fold = jnp.where((lax.broadcasted_iota(jnp.int32, (8, 128), 1) >> 4) == row, 1.0, 0.0).astype(BF)
    trades = [
        remote(pick_ref.at[1], y_ref.at[0], y_send.at[0], y_recv.at[0], ring_y[0]),
        remote(pick_ref.at[0], y_ref.at[1], y_send.at[1], y_recv.at[1], ring_y[1]),
        remote(pick_ref.at[0], y_ref.at[2], y_send.at[2], y_recv.at[2], ring_y[2]),
    ]
    for own in range(2):
        base = (h if own else 1 - h) * 128

        def pick(i, carry):
            q = idx_ref[base + (i & 15) * 8 + (i >> 4)]
            p = q >> 4
            c = jnp.where((p >> 6) == yh, q & 15, 99)
            v = jnp.where(lane_c == c, a_ref[(p & 1) * 32 + ((p & 63) >> 1)], 0.0)
            gm_ref[own, pl.ds(pl.multiple_of(8 * i, 8), 8), :] = v
            return carry

        lax.fori_loop(0, 128, pick, 0, unroll=16)
        got = []
        for t in range(8):
            v = gm_ref[own, 128 * t : 128 * (t + 1), :]
            hi = v.astype(BF)
            rest = v - hi.astype(F32)
            mid = rest.astype(BF)
            lo = (rest - mid.astype(F32)).astype(BF)
            got.append(dot(fold, hi, 1, 1) + dot(fold, mid, 1, 1) + dot(fold, lo, 1, 1))
        for bit in range(3):
            got = swap(got, bit, lax.broadcasted_iota(jnp.int32, (8, 128), 1))
        for e in range(8):
            pick_ref[own, 8 * e : 8 * (e + 1), :] = got[e]
        if own:
            trades[0].start()
        else:
            trades[2].start()
            trades[1].start()
    for t in trades:
        t.wait()
    own = pick_ref[1] + y_ref[0]
    other = y_ref[1] + y_ref[2]
    for f2 in range(2):
        g_ref[j, f2, 0] = own[32 * f2 : 32 * f2 + 32]
        g_ref[j, f2, 1] = other[32 * f2 : 32 * f2 + 32]

    sign = 1 - 2 * k

    def source(dz, dx):
        return zat(-sign * dz) * NX + xat(-sign * dx)

    def pass_on(u2, f2, targets):
        blk = g_ref.at[k * 32 + u2, f2]
        devices = [device(zat(sign * dz), xat(sign * dx), k) for dz, dx in targets] + [device(z, x, 1 - k)]
        for dev in devices:
            remote(blk, blk, g_send, g_recv.at[k * 32 + u2, f2], dev).start()

    def arrived(kk, u2, f2):
        blk = g_ref.at[kk * 32 + u2, f2]
        remote(blk, blk, g_send, g_recv.at[kk * 32 + u2, f2], ring_y[0]).wait_recv()

    def cross(*us):
        for u2 in us:
            for f2 in range(2):
                arrived(1 - k, u2, f2)
        for u2 in us:
            blocks = []
            for f2 in range(2):
                blocks += [g_ref[u2, f2].reshape(64, 128), g_ref[32 + u2, f2].reshape(64, 128)]
            hi, lo = split(jnp.concatenate(blocks, axis=0))
            res = dot(lhs_ref[u2], jnp.concatenate((hi, lo), axis=1), 1, 0)
            res = res[:128, :128] + (res[:128, 128:] + res[128:, :128])
            at = pl.ds(pl.multiple_of(8 * u2, 8), 8)
            for c in range(16):
                x_ref[c, at, :] = res[8 * c : 8 * c + 8]

    ready = []
    for f2 in range(2):
        pass_on(u, f2, FIRST[f2])
    for f2, dz, dx, targets in GATHER:
        u2 = source(dz, dx)
        if targets is None:
            ready.append(u2)
            if len(ready) == 2:
                cross(*ready)
                ready = []
        else:
            arrived(k, u2, f2)
            pass_on(u2, f2, targets)
    most_g = g_ref.at[pl.ds(0, NJ - 1)]
    remote(most_g, most_g, g_send, a_recv, ring_y[0]).wait_send()
    some_a.wait_send()
    sent_z = w_ref.at[pl.ds(0, 448)]
    remote(sent_z, sent_z, z_send, a_recv, ring_y[0]).wait_send()


def output_kernel(x_ref, hi_hbm, lo_hbm, out_ref, hi_ref, lo_ref, mix_ref, stage_ref, load, sem):
    loads = [
        pltpu.make_async_copy(hi_hbm, hi_ref, load.at[0]),
        pltpu.make_async_copy(lo_hbm, lo_ref, load.at[1]),
    ]
    for c in loads:
        c.start()
    for c in range(16):
        t = x_ref[c].T
        for half in range(2):
            mix_ref[half, pl.ds(c, 128, stride=16), :] = t[:, 128 * half : 128 * half + 128]
    copies = []
    for m in range(8):
        parts = [split(mix_ref[half, 256 * m : 256 * m + 256, :]) for half in range(2)]
        hi = jnp.concatenate([p[0] for p in parts], axis=1)
        lo = jnp.concatenate([p[1] for p in parts], axis=1)
        if m == 0:
            for c in loads:
                c.wait()
        both = dot(jnp.concatenate((hi, lo), axis=0), hi_ref[...], 1, 0)
        stage_ref[m] = both[:256] + (both[256:] + dot(hi, lo_ref[...], 1, 0))
        copy = pltpu.make_async_copy(stage_ref.at[m], out_ref.at[pl.ds(256 * m, 256)], sem.at[m])
        copy.start()
        copies.append(copy)
    for copy in copies:
        copy.wait()


def body(recording, source_channels):
    fwd_hi, fwd_lo = (jnp.asarray(t) for t in split_np(forward_table()))
    inv_hi, inv_lo = (jnp.asarray(t) for t in split_np(inverse_table()))
    dma = pltpu.SemaphoreType.DMA
    cross = pl.pallas_call(
        exchange_kernel,
        out_shape=pltpu.VMEM((16, 256, 128), F32),
        in_specs=[HBM] * 4,
        out_specs=VMEM,
        scratch_shapes=[
            pltpu.SMEM((256,), jnp.int32),
            pltpu.VMEM((256, L), F32),
            pltpu.VMEM((256, L), BF),
            pltpu.VMEM((256, L), BF),
            pltpu.VMEM((512, 128), F32),
            pltpu.VMEM((512, 128), F32),
            pltpu.VMEM((2, NZ, 32, 128), F32),
            pltpu.VMEM((NJ, 8, 128), F32),
            pltpu.VMEM((2, 1024, 128), F32),
            pltpu.VMEM((2, 64, 128), F32),
            pltpu.VMEM((3, 64, 128), F32),
            pltpu.VMEM((NJ, 2, 2, 32, 128), F32),
            pltpu.VMEM((2, 32, 16, 128), F32),
            pltpu.VMEM((32, 256, 256), BF),
            dma((4,)), dma, dma((2, NZ)), dma, dma, dma((3,)), dma((3,)), dma, dma, dma, dma((NJ, 2)),
        ],
        compiler_params=pltpu.CompilerParams(collective_id=0, has_side_effects=True),
        name="exchange",
    )(source_channels, recording.reshape(256, L), fwd_hi, fwd_lo)
    out = pl.pallas_call(
        output_kernel,
        out_shape=jax.ShapeDtypeStruct((2048, LAGS), F32),
        in_specs=[VMEM, ANY, ANY],
        out_specs=ANY,
        scratch_shapes=[
            pltpu.VMEM((256, LAGS), BF),
            pltpu.VMEM((256, LAGS), BF),
            pltpu.VMEM((2, 2048, 128), F32),
            pltpu.VMEM((8, 256, LAGS), F32),
            dma((2,)),
            dma((8,)),
        ],
        compiler_params=pltpu.CompilerParams(vmem_limit_bytes=24 << 20),
        name="correlate",
    )(cross, inv_hi, inv_lo)
    return out.reshape(128, 16, LAGS)


def solution(mesh):
    return jax.shard_map(
        body,
        mesh=mesh,
        in_specs=(P("half", "shard", None), P()),
        out_specs=P("half", "shard", None),
        check_vma=False,
    )
```

```python
import functools

import jax
import jax.numpy as jnp
import numpy as np
from jax import lax
from jax.experimental import pallas as pl
from jax.experimental.pallas import tpu as pltpu
from jax.sharding import PartitionSpec as P

F = 128
L = 1024
LAGS = 512
SEG = 32
water_level = 0.2
epsilon = 1e-05

NX, NZ = 4, 8
NJ = 64
ANY = pl.BlockSpec(memory_space=pl.ANY)
VMEM = pl.BlockSpec(memory_space=pltpu.VMEM)
HBM = pl.BlockSpec(memory_space=pltpu.HBM)
MESH = pl.DeviceIdType.MESH
BF = jnp.bfloat16
F32 = jnp.float32


def split_np(table):
    hi = table.astype(np.float32).astype(jnp.bfloat16)
    lo = (table - hi.astype(np.float64)).astype(np.float32).astype(jnp.bfloat16)
    return hi, lo


def forward_table():
    bins = np.arange(F) + 1
    times = np.arange(L)
    angle = 2.0 * np.pi * (bins[:, None] * times[None, :] % L) / L
    taper = 0.5 - 0.5 * np.cos(2.0 * np.pi * times / L)
    return np.concatenate((np.cos(angle) * taper, -np.sin(angle) * taper), axis=0)


def inverse_table():
    bins = np.arange(F) + 1
    shifts = np.arange(LAGS) - LAGS // 2
    angle = 2.0 * np.pi * (bins[:, None] * shifts[None, :] % L) / L
    table = np.stack((np.cos(angle), -np.sin(angle)), axis=1) / np.sqrt(SEG * F)
    return table.reshape(2, 32, 2, 2, LAGS).transpose(1, 2, 0, 3, 4).reshape(2 * F, LAGS)


def split(v):
    hi = v.astype(BF)
    return hi, (v - hi.astype(F32)).astype(BF)


def dot(a, b, ca, cb):
    return lax.dot_general(a, b, (((ca,), (cb,)), ((), ())), preferred_element_type=F32)


OFF_Z = (1, -1, 2, -2, 3, -3, 4)
FIRST = (
    ((-1, 0), (2, 0), (0, -2), (4, 0)),
    ((0, 1), (0, -1), (2, 0)),
)
GATHER = (
    (0, 0, 0, None, 0), (0, -1, 0, ((0, 1), (-1, 0), (0, -1)), 1), (1, 0, 1, ((-3, 0), (1, 0)), 0),
    (1, 0, -1, ((0, -1),), 0), (0, 0, 2, ((1, 0), (0, 1)), 0), (0, 2, 0, ((0, -2), (0, 1), (0, -1)), 0),
    (1, 2, 0, ((1, 0),), 0), (0, -1, 1, ((0, 1), (1, 0)), 0), (0, -2, 0, ((-1, 0), (0, 1)), 1),
    (0, -1, -1, ((-1, 0),), 0), (1, 0, 2, ((-1, 0),), 0), (1, -1, 0, (), 0), (1, 1, 1, ((1, 0), (0, -1)), 0),
    (0, 0, -1, (), 0), (0, 4, 0, ((0, 1), (0, -1)), 1), (0, 0, 2, None, 0), (0, 2, 1, ((1, 0),), 0),
    (0, 1, 2, ((0, 1), (0, -1)), 1), (0, 2, -1, (), 1), (1, 3, 0, ((0, -1), (0, 1)), 0),
    (0, 2, 2, ((1, 0), (2, 0)), 1), (1, -3, 1, ((0, 1), (1, 0), (0, -1)), 0), (0, -1, 2, ((-1, 0),), 0),
    (0, 0, 1, (), 0), (0, 0, 1, None, 0), (0, -2, 1, (), 0), (0, -2, -1, (), 1), (1, 1, 0, (), 0), (1, -2, 0, (), 0),
    (0, -3, 0, ((-2, 0), (0, -1)), 0), (0, 4, 1, ((1, 0),), 0), (1, -1, 2, ((0, -1), (0, 1)), 0), (0, 0, -1, None, 0),
    (0, 4, -1, ((-1, 0),), 1), (1, 2, 1, ((2, 0),), 0), (1, 4, 0, (), 0), (0, 1, -1, ((0, 1),), 1), (0, 3, 1, (), 0),
    (0, 1, 1, (), 0), (0, 3, 2, (), 0), (1, 1, 2, (), 0), (0, 1, 2, None, 0), (1, 3, -1, ((0, -1),), 0),
    (1, 3, 1, (), 0), (1, -2, 1, ((0, 1),), 0), (1, 2, -1, (), 0), (1, -3, 2, ((0, 1), (-1, 0)), 0),
    (0, -2, 2, ((-1, 0),), 0), (1, -3, 0, (), 0), (0, 4, 2, (), 0), (1, 2, 2, (), 0), (0, -3, -1, (), 0),
    (1, -1, 1, (), 0), (0, 2, 0, None, 0), (0, 4, 0, None, 0), (0, 2, -1, None, 0), (1, -2, -1, (), 0),
    (1, -1, -1, (), 0), (0, -1, -1, None, 0), (0, -3, 1, (), 0), (0, 1, 0, (), 0), (0, -1, 2, None, 0),
    (0, 1, 0, None, 0), (0, -2, 1, None, 0), (0, 3, -1, (), 0), (1, 4, -1, (), 0), (0, 3, 0, (), 0), (1, 3, 2, (), 0),
    (0, 3, 0, None, 0), (1, 4, 1, (), 0), (1, -2, 2, (), 0), (0, 1, 1, None, 0), (1, 1, -1, (), 0),
    (1, -3, -1, (), 0), (1, 4, 2, (), 0), (0, -3, -1, None, 0), (0, -3, 2, (), 0), (0, -3, 1, None, 0),
    (0, 3, -1, None, 0), (0, -2, 2, None, 0), (0, -1, 0, None, 0), (0, -3, 0, None, 0), (0, -3, 2, None, 0),
    (0, 4, -1, None, 0), (0, 2, 1, None, 0), (0, 4, 1, None, 0), (0, 2, 2, None, 0), (0, 3, 1, None, 0),
    (0, 4, 2, None, 0), (0, -1, 1, None, 0), (0, 3, 2, None, 0), (0, -2, 0, None, 0), (0, -2, -1, None, 0),
    (0, 1, -1, None, 0),
)


def whiten(rec_ref, hi_ref, lo_ref, out_ref):
    rec_hi, rec_lo = split(rec_ref[...])
    spec = dot(hi_ref[...], rec_hi, 1, 1) + dot(hi_ref[...], rec_lo, 1, 1) + dot(lo_ref[...], rec_hi, 1, 1)
    re, im = spec[:F], spec[F:]
    mag = jnp.sqrt(re * re + im * im)
    zeros = jnp.zeros((2, mag.shape[1]), F32)
    pad = jnp.concatenate((zeros, mag, zeros), axis=0)
    smooth = pad[0:F]
    for off in range(1, 5):
        smooth = smooth + pad[off : off + F]
    mean = jnp.sum(mag, axis=0, keepdims=True) * (1.0 / F)
    divisor = smooth / 5.0 + water_level * mean + epsilon
    for q, part in enumerate((re, im)):
        white = part / divisor
        for s_hi in range(2):
            out_ref[pl.ds(2 * q + s_hi, F, stride=4), :] = white[:, 128 * s_hi : 128 * (s_hi + 1)]


def swap(v, bit, lane):
    step = 1 << bit
    low = (lane & step) == 0
    v = list(v)
    for i in range(len(v)):
        if i & step:
            continue
        a, b = v[i], v[i + step]
        v[i] = jnp.where(low, a, pltpu.roll(b, step, 1))
        v[i + step] = jnp.where(low, pltpu.roll(a, 128 - step, 1), b)
    return v


def lanes():
    return lax.broadcasted_iota(jnp.int32, (16, 128), 1)


def receivers_first(ref, mid_ref, side):
    v = []
    for e in range(4):
        t = ref[pl.ds(e, F, stride=4), :].T
        v += [t[16 * i : 16 * i + 16] for i in range(8)]
    for bit in range(5):
        v = swap(v, bit, lanes())
    for i in range(32):
        mid_ref[side, i] = v[i]


def receivers_last(mid_ref, lhs_ref):
    lane = lanes()
    first = (lane & 16) == 0
    low = (lane & 32) == 0
    row8 = lax.broadcasted_iota(jnp.int32, (8, 128), 0)
    lane8 = lax.broadcasted_iota(jnp.int32, (8, 128), 1)
    imag = (row8 & 1) == 1
    same = ((row8 >> 1) & 1) == (lane8 >> 6)
    keep = [same & ((row8 >> 2) == f2) for f2 in range(2)]
    for i in range(32):
        a, b = mid_ref[0, i], mid_ref[1, i]
        pair = (jnp.where(low, a, pltpu.roll(b, 32, 1)), jnp.where(low, pltpu.roll(a, 96, 1), b))
        for half in range(2):
            g = 32 * half + i
            u, f2 = g // 2, g % 2
            re = pair[half]
            im = jnp.where(first, pltpu.roll(re, 112, 1), -pltpu.roll(re, 16, 1))
            rows = []
            for c in range(16):
                v = jnp.where(
                    imag, jnp.broadcast_to(im[c : c + 1], (8, 128)), jnp.broadcast_to(re[c : c + 1], (8, 128))
                )
                rows.append(jnp.where(keep[f2], v, 0.0))
            hi, lo = split(jnp.concatenate(rows, axis=0))
            lhs_ref[u, 0:128, 128 * f2 : 128 * f2 + 128] = hi
            lhs_ref[u, 128:256, 128 * f2 : 128 * f2 + 128] = lo


def exchange_kernel(idx_hbm, rec_hbm, hi_hbm, lo_hbm, x_ref, idx_ref, rec_ref, hi_ref, lo_ref, w_ref, wo_ref, z_ref, a_ref,
                    gm_ref, pick_ref, y_ref, g_ref, mid_ref, lhs_ref,
                    load, z_send, z_recv, a_send, a_recv, y_send, y_recv, wo_send, wo_recv, g_send, g_recv):
    h = lax.axis_index("half")
    s = lax.axis_index("shard")
    yh, u, k = s // NJ, (s % NJ) // 2, s % 2
    z, x = u // NX, u % NX
    j = k * 32 + u

    def device(zz, xx, kk):
        return (h, yh * NJ + (zz * NX + xx) * 2 + kk)

    def zat(d):
        return (z + d + NZ) % NZ

    def xat(d):
        return (x + d + NX) % NX

    def remote(src, dst, ssem, rsem, dev):
        return pltpu.make_async_remote_copy(
            src_ref=src, dst_ref=dst, send_sem=ssem, recv_sem=rsem, device_id=dev, device_id_type=MESH
        )

    plane = [(xat(d), kk) for d in (0, 1, -1, 2) for kk in (k, 1 - k)][1:]
    ring_y = [(h, (1 - yh) * NJ + s % NJ), (1 - h, s), (1 - h, (1 - yh) * NJ + s % NJ)]
    barrier = pltpu.get_barrier_semaphore()
    for dev in [device(zat(d), x, k) for d in OFF_Z] + [device(z, *p) for p in plane] + ring_y:
        pl.semaphore_signal(barrier, inc=1, device_id=dev, device_id_type=MESH)
    loads = [
        pltpu.make_async_copy(a, b, load.at[i])
        for i, (a, b) in enumerate(((rec_hbm, rec_ref), (hi_hbm, hi_ref), (lo_hbm, lo_ref), (idx_hbm, idx_ref)))
    ]
    for c in loads:
        c.start()
    for c in loads:
        c.wait()
    whiten(rec_ref, hi_ref, lo_ref, w_ref)
    pl.semaphore_wait(barrier, 17)

    def rows(kk, zz, n):
        return pl.ds(pl.multiple_of((kk * 32 + zz * NX) * 8, 8), n)

    for d in OFF_Z:
        for kk in range(2):
            remote(
                w_ref.at[rows(kk, zat(d), 32)], z_ref.at[kk, z], z_send, z_recv.at[kk, z], device(zat(d), x, k)
            ).start()
    wo = remote(w_ref, wo_ref, wo_send, wo_recv, ring_y[1])
    wo.start()
    for kk in range(2):
        z_ref[kk, z] = w_ref[rows(kk, z, 32), :]
    receivers_first(w_ref, mid_ref, 0)
    for d in (0,) + OFF_Z:
        zs = zat(d)
        if d:
            for kk in range(2):
                remote(z_ref.at[kk, zs], z_ref.at[kk, zs], z_send, z_recv.at[kk, zs], ring_y[0]).wait_recv()
        mine = k * 32 + zs * NX + x
        for xx, kk in plane:
            src = z_ref.at[kk, zs, pl.ds(pl.multiple_of(xx * 8, 8), 8)]
            remote(src, a_ref.at[mine], a_send, a_recv, device(z, xx, kk)).start()
        a_ref[mine] = z_ref[k, zs, pl.ds(pl.multiple_of(x * 8, 8), 8), :]
    wo.wait()
    receivers_first(wo_ref, mid_ref, 1)
    receivers_last(mid_ref, lhs_ref)
    some_a = remote(a_ref.at[pl.ds(0, 56)], a_ref.at[pl.ds(0, 56)], a_send, a_recv, ring_y[0])
    some_a.wait_recv()

    lane_c = lax.broadcasted_iota(jnp.int32, (8, 128), 1) & 15

    row = lax.broadcasted_iota(jnp.int32, (8, 128), 0)
    fold = jnp.where((lax.broadcasted_iota(jnp.int32, (8, 128), 1) >> 4) == row, 1.0, 0.0).astype(BF)
    trades = [
        remote(pick_ref.at[1], y_ref.at[0], y_send.at[0], y_recv.at[0], ring_y[0]),
        remote(pick_ref.at[0], y_ref.at[1], y_send.at[1], y_recv.at[1], ring_y[1]),
        remote(pick_ref.at[0], y_ref.at[2], y_send.at[2], y_recv.at[2], ring_y[2]),
    ]
    for own in range(2):
        base = (h if own else 1 - h) * 128

        def pick(i, carry):
            q = idx_ref[base + (i & 15) * 8 + (i >> 4)]
            p = q >> 4
            c = jnp.where((p >> 6) == yh, q & 15, 99)
            v = jnp.where(lane_c == c, a_ref[(p & 1) * 32 + ((p & 63) >> 1)], 0.0)
            gm_ref[own, pl.ds(pl.multiple_of(8 * i, 8), 8), :] = v
            return carry

        lax.fori_loop(0, 128, pick, 0, unroll=16)
        got = []
        for t in range(8):
            v = gm_ref[own, 128 * t : 128 * (t + 1), :]
            hi = v.astype(BF)
            rest = v - hi.astype(F32)
            mid = rest.astype(BF)
            lo = (rest - mid.astype(F32)).astype(BF)
            got.append(dot(fold, hi, 1, 1) + dot(fold, mid, 1, 1) + dot(fold, lo, 1, 1))
        for bit in range(3):
            got = swap(got, bit, lax.broadcasted_iota(jnp.int32, (8, 128), 1))
        for e in range(8):
            pick_ref[own, 8 * e : 8 * (e + 1), :] = got[e]
        if own:
            trades[0].start()
        else:
            trades[2].start()
            trades[1].start()
    for t in trades:
        t.wait()
    own = pick_ref[1] + y_ref[0]
    other = y_ref[1] + y_ref[2]
    for f2 in range(2):
        g_ref[j, f2, 0] = own[32 * f2 : 32 * f2 + 32]
        g_ref[j, f2, 1] = other[32 * f2 : 32 * f2 + 32]

    sign = 1 - 2 * k

    def source(dz, dx):
        return zat(-sign * dz) * NX + xat(-sign * dx)

    def pass_on(u2, f2, targets, over_y=False):
        blk = g_ref.at[k * 32 + u2, f2]
        devices = [device(zat(sign * dz), xat(sign * dx), k) for dz, dx in targets] + [device(z, x, 1 - k)]
        if over_y:
            devices.append(ring_y[0])
        for dev in devices:
            remote(blk, blk, g_send, g_recv.at[k * 32 + u2, f2], dev).start()

    def arrived(kk, u2, f2):
        blk = g_ref.at[kk * 32 + u2, f2]
        remote(blk, blk, g_send, g_recv.at[kk * 32 + u2, f2], ring_y[0]).wait_recv()

    def cross(*us):
        for u2 in us:
            for f2 in range(2):
                arrived(1 - k, u2, f2)
        for u2 in us:
            blocks = []
            for f2 in range(2):
                blocks += [g_ref[u2, f2].reshape(64, 128), g_ref[32 + u2, f2].reshape(64, 128)]
            hi, lo = split(jnp.concatenate(blocks, axis=0))
            res = dot(lhs_ref[u2], jnp.concatenate((hi, lo), axis=1), 1, 0)
            res = res[:128, :128] + (res[:128, 128:] + res[128:, :128])
            at = pl.ds(pl.multiple_of(8 * u2, 8), 8)
            for c in range(16):
                x_ref[c, at, :] = res[8 * c : 8 * c + 8]

    ready = []
    for tree in range(2):
        pass_on(u, (tree + yh) % 2, FIRST[tree])
    for tree, dz, dx, targets, over_y in GATHER:
        u2, f2 = source(dz, dx), (tree + yh) % 2
        if targets is None:
            ready.append(u2)
            if len(ready) == 4:
                cross(*ready)
                ready = []
        else:
            arrived(k, u2, f2)
            pass_on(u2, f2, targets, over_y)
    most_g = g_ref.at[pl.ds(0, NJ - 1)]
    remote(most_g, most_g, g_send, a_recv, ring_y[0]).wait_send()
    some_a.wait_send()
    sent_z = w_ref.at[pl.ds(0, 448)]
    remote(sent_z, sent_z, z_send, a_recv, ring_y[0]).wait_send()


def output_kernel(x_ref, hi_hbm, lo_hbm, out_ref, hi_ref, lo_ref, mix_ref, stage_ref, load, sem):
    loads = [
        pltpu.make_async_copy(hi_hbm, hi_ref, load.at[0]),
        pltpu.make_async_copy(lo_hbm, lo_ref, load.at[1]),
    ]
    for c in loads:
        c.start()
    for c in range(16):
        t = x_ref[c].T
        for half in range(2):
            mix_ref[half, pl.ds(c, 128, stride=16), :] = t[:, 128 * half : 128 * half + 128]
    copies = []
    for m in range(8):
        parts = [split(mix_ref[half, 256 * m : 256 * m + 256, :]) for half in range(2)]
        hi = jnp.concatenate([p[0] for p in parts], axis=1)
        lo = jnp.concatenate([p[1] for p in parts], axis=1)
        if m == 0:
            for c in loads:
                c.wait()
        both = dot(jnp.concatenate((hi, lo), axis=0), hi_ref[...], 1, 0)
        stage_ref[m] = both[:256] + (both[256:] + dot(hi, lo_ref[...], 1, 0))
        copy = pltpu.make_async_copy(stage_ref.at[m], out_ref.at[pl.ds(256 * m, 256)], sem.at[m])
        copy.start()
        copies.append(copy)
    for copy in copies:
        copy.wait()


def body(recording, source_channels):
    fwd_hi, fwd_lo = (jnp.asarray(t) for t in split_np(forward_table()))
    inv_hi, inv_lo = (jnp.asarray(t) for t in split_np(inverse_table()))
    dma = pltpu.SemaphoreType.DMA
    cross = pl.pallas_call(
        exchange_kernel,
        out_shape=pltpu.VMEM((16, 256, 128), F32),
        in_specs=[HBM] * 4,
        out_specs=VMEM,
        scratch_shapes=[
            pltpu.SMEM((256,), jnp.int32),
            pltpu.VMEM((256, L), F32),
            pltpu.VMEM((256, L), BF),
            pltpu.VMEM((256, L), BF),
            pltpu.VMEM((512, 128), F32),
            pltpu.VMEM((512, 128), F32),
            pltpu.VMEM((2, NZ, 32, 128), F32),
            pltpu.VMEM((NJ, 8, 128), F32),
            pltpu.VMEM((2, 1024, 128), F32),
            pltpu.VMEM((2, 64, 128), F32),
            pltpu.VMEM((3, 64, 128), F32),
            pltpu.VMEM((NJ, 2, 2, 32, 128), F32),
            pltpu.VMEM((2, 32, 16, 128), F32),
            pltpu.VMEM((32, 256, 256), BF),
            dma((4,)), dma, dma((2, NZ)), dma, dma, dma((3,)), dma((3,)), dma, dma, dma, dma((NJ, 2)),
        ],
        compiler_params=pltpu.CompilerParams(collective_id=0, has_side_effects=True),
        name="exchange",
    )(source_channels, recording.reshape(256, L), fwd_hi, fwd_lo)
    out = pl.pallas_call(
        output_kernel,
        out_shape=jax.ShapeDtypeStruct((2048, LAGS), F32),
        in_specs=[VMEM, ANY, ANY],
        out_specs=ANY,
        scratch_shapes=[
            pltpu.VMEM((256, LAGS), BF),
            pltpu.VMEM((256, LAGS), BF),
            pltpu.VMEM((2, 2048, 128), F32),
            pltpu.VMEM((8, 256, LAGS), F32),
            dma((2,)),
            dma((8,)),
        ],
        compiler_params=pltpu.CompilerParams(vmem_limit_bytes=24 << 20),
        name="correlate",
    )(cross, inv_hi, inv_lo)
    return out.reshape(128, 16, LAGS)


def solution(mesh):
    return jax.shard_map(
        body,
        mesh=mesh,
        in_specs=(P("half", "shard", None), P()),
        out_specs=P("half", "shard", None),
        check_vma=False,
    )
```

```python
import functools

import jax
import jax.numpy as jnp
import numpy as np
from jax import lax
from jax.experimental import pallas as pl
from jax.experimental.pallas import tpu as pltpu
from jax.sharding import PartitionSpec as P

F = 128
L = 1024
LAGS = 512
SEG = 32
water_level = 0.2
epsilon = 1e-05

NX, NZ = 4, 8
NJ = 64
ANY = pl.BlockSpec(memory_space=pl.ANY)
VMEM = pl.BlockSpec(memory_space=pltpu.VMEM)
HBM = pl.BlockSpec(memory_space=pltpu.HBM)
MESH = pl.DeviceIdType.MESH
BF = jnp.bfloat16
F32 = jnp.float32


def split_np(table):
    hi = table.astype(np.float32).astype(jnp.bfloat16)
    lo = (table - hi.astype(np.float64)).astype(np.float32).astype(jnp.bfloat16)
    return hi, lo


def forward_table():
    bins = np.arange(F) + 1
    times = np.arange(L)
    angle = 2.0 * np.pi * (bins[:, None] * times[None, :] % L) / L
    taper = 0.5 - 0.5 * np.cos(2.0 * np.pi * times / L)
    return np.concatenate((np.cos(angle) * taper, -np.sin(angle) * taper), axis=0)


def inverse_table():
    bins = np.arange(F) + 1
    shifts = np.arange(LAGS) - LAGS // 2
    angle = 2.0 * np.pi * (bins[:, None] * shifts[None, :] % L) / L
    table = np.stack((np.cos(angle), -np.sin(angle)), axis=1) / np.sqrt(SEG * F)
    return table.reshape(2, 32, 2, 2, LAGS).transpose(1, 2, 0, 3, 4).reshape(2 * F, LAGS)


def split(v):
    hi = v.astype(BF)
    return hi, (v - hi.astype(F32)).astype(BF)


def dot(a, b, ca, cb):
    return lax.dot_general(a, b, (((ca,), (cb,)), ((), ())), preferred_element_type=F32)


OFF_Z = (4, 3, -3, 2, -2, 1, -1)
FIRST = (
    ((-1, 0), (2, 0), (0, -2), (4, 0)),
    ((0, 1), (0, -1), (2, 0)),
)
GATHER = (
    (0, 0, 0, None, 0), (0, -1, 0, ((0, 1), (-1, 0), (0, -1)), 1), (1, 0, 1, ((-3, 0), (1, 0)), 0),
    (1, 0, -1, ((0, -1),), 0), (0, 0, 2, ((1, 0), (0, 1)), 0), (0, 2, 0, ((0, -2), (0, 1), (0, -1)), 0),
    (1, 2, 0, ((1, 0),), 0), (0, -1, 1, ((0, 1), (1, 0)), 0), (0, -2, 0, ((-1, 0), (0, 1)), 1),
    (0, -1, -1, ((-1, 0),), 0), (1, 0, 2, ((-1, 0),), 0), (1, -1, 0, (), 0), (1, 1, 1, ((1, 0), (0, -1)), 0),
    (0, 0, -1, (), 0), (0, 4, 0, ((0, 1), (0, -1)), 1), (0, 0, 2, None, 0), (0, 2, 1, ((1, 0),), 0),
    (0, 1, 2, ((0, 1), (0, -1)), 1), (0, 2, -1, (), 1), (1, 3, 0, ((0, -1), (0, 1)), 0),
    (0, 2, 2, ((1, 0), (2, 0)), 1), (1, -3, 1, ((0, 1), (1, 0), (0, -1)), 0), (0, -1, 2, ((-1, 0),), 0),
    (0, 0, 1, (), 0), (0, 0, 1, None, 0), (0, -2, 1, (), 0), (0, -2, -1, (), 1), (1, 1, 0, (), 0), (1, -2, 0, (), 0),
    (0, -3, 0, ((-2, 0), (0, -1)), 0), (0, 4, 1, ((1, 0),), 0), (1, -1, 2, ((0, -1), (0, 1)), 0), (0, 0, -1, None, 0),
    (0, 4, -1, ((-1, 0),), 1), (1, 2, 1, ((2, 0),), 0), (1, 4, 0, (), 0), (0, 1, -1, ((0, 1),), 1), (0, 3, 1, (), 0),
    (0, 1, 1, (), 0), (0, 3, 2, (), 0), (1, 1, 2, (), 0), (0, 1, 2, None, 0), (1, 3, -1, ((0, -1),), 0),
    (1, 3, 1, (), 0), (1, -2, 1, ((0, 1),), 0), (1, 2, -1, (), 0), (1, -3, 2, ((0, 1), (-1, 0)), 0),
    (0, -2, 2, ((-1, 0),), 0), (1, -3, 0, (), 0), (0, 4, 2, (), 0), (1, 2, 2, (), 0), (0, -3, -1, (), 0),
    (1, -1, 1, (), 0), (0, 2, 0, None, 0), (0, 4, 0, None, 0), (0, 2, -1, None, 0), (1, -2, -1, (), 0),
    (1, -1, -1, (), 0), (0, -1, -1, None, 0), (0, -3, 1, (), 0), (0, 1, 0, (), 0), (0, -1, 2, None, 0),
    (0, 1, 0, None, 0), (0, -2, 1, None, 0), (0, 3, -1, (), 0), (1, 4, -1, (), 0), (0, 3, 0, (), 0), (1, 3, 2, (), 0),
    (0, 3, 0, None, 0), (1, 4, 1, (), 0), (1, -2, 2, (), 0), (0, 1, 1, None, 0), (1, 1, -1, (), 0),
    (1, -3, -1, (), 0), (1, 4, 2, (), 0), (0, -3, -1, None, 0), (0, -3, 2, (), 0), (0, -3, 1, None, 0),
    (0, 3, -1, None, 0), (0, -2, 2, None, 0), (0, -1, 0, None, 0), (0, -3, 0, None, 0), (0, -3, 2, None, 0),
    (0, 4, -1, None, 0), (0, 2, 1, None, 0), (0, 4, 1, None, 0), (0, 2, 2, None, 0), (0, 3, 1, None, 0),
    (0, 4, 2, None, 0), (0, -1, 1, None, 0), (0, 3, 2, None, 0), (0, -2, 0, None, 0), (0, -2, -1, None, 0),
    (0, 1, -1, None, 0),
)


def whiten(rec_ref, hi_ref, lo_ref, out_ref):
    rec_hi, rec_lo = split(rec_ref[...])
    spec = dot(hi_ref[...], rec_hi, 1, 1) + dot(hi_ref[...], rec_lo, 1, 1) + dot(lo_ref[...], rec_hi, 1, 1)
    re, im = spec[:F], spec[F:]
    mag = jnp.sqrt(re * re + im * im)
    zeros = jnp.zeros((2, mag.shape[1]), F32)
    pad = jnp.concatenate((zeros, mag, zeros), axis=0)
    smooth = pad[0:F]
    for off in range(1, 5):
        smooth = smooth + pad[off : off + F]
    mean = jnp.sum(mag, axis=0, keepdims=True) * (1.0 / F)
    divisor = smooth / 5.0 + water_level * mean + epsilon
    for q, part in enumerate((re, im)):
        white = part / divisor
        for s_hi in range(2):
            out_ref[pl.ds(2 * q + s_hi, F, stride=4), :] = white[:, 128 * s_hi : 128 * (s_hi + 1)]


def swap(v, bit, lane):
    step = 1 << bit
    low = (lane & step) == 0
    v = list(v)
    for i in range(len(v)):
        if i & step:
            continue
        a, b = v[i], v[i + step]
        v[i] = jnp.where(low, a, pltpu.roll(b, step, 1))
        v[i + step] = jnp.where(low, pltpu.roll(a, 128 - step, 1), b)
    return v


def lanes():
    return lax.broadcasted_iota(jnp.int32, (16, 128), 1)


def receivers_first(ref, mid_ref, side):
    v = []
    for e in range(4):
        t = ref[pl.ds(e, F, stride=4), :].T
        v += [t[16 * i : 16 * i + 16] for i in range(8)]
    for bit in range(5):
        v = swap(v, bit, lanes())
    for i in range(32):
        mid_ref[side, i] = v[i]


def receivers_last(mid_ref, lhs_ref):
    lane = lanes()
    first = (lane & 16) == 0
    low = (lane & 32) == 0
    row8 = lax.broadcasted_iota(jnp.int32, (8, 128), 0)
    lane8 = lax.broadcasted_iota(jnp.int32, (8, 128), 1)
    imag = (row8 & 1) == 1
    same = ((row8 >> 1) & 1) == (lane8 >> 6)
    keep = [same & ((row8 >> 2) == f2) for f2 in range(2)]
    for i in range(32):
        a, b = mid_ref[0, i], mid_ref[1, i]
        pair = (jnp.where(low, a, pltpu.roll(b, 32, 1)), jnp.where(low, pltpu.roll(a, 96, 1), b))
        for half in range(2):
            g = 32 * half + i
            u, f2 = g // 2, g % 2
            re = pair[half]
            im = jnp.where(first, pltpu.roll(re, 112, 1), -pltpu.roll(re, 16, 1))
            rows = []
            for c in range(16):
                v = jnp.where(
                    imag, jnp.broadcast_to(im[c : c + 1], (8, 128)), jnp.broadcast_to(re[c : c + 1], (8, 128))
                )
                rows.append(jnp.where(keep[f2], v, 0.0))
            hi, lo = split(jnp.concatenate(rows, axis=0))
            lhs_ref[u, 0:128, 128 * f2 : 128 * f2 + 128] = hi
            lhs_ref[u, 128:256, 128 * f2 : 128 * f2 + 128] = lo


def exchange_kernel(idx_hbm, rec_hbm, hi_hbm, lo_hbm, x_ref, idx_ref, rec_ref, hi_ref, lo_ref, w_ref, wo_ref, z_ref, a_ref,
                    gm_ref, pick_ref, y_ref, g_ref, mid_ref, lhs_ref,
                    load, z_send, z_recv, a_send, a_recv, y_send, y_recv, wo_send, wo_recv, g_send, g_recv):
    h = lax.axis_index("half")
    s = lax.axis_index("shard")
    yh, u, k = s // NJ, (s % NJ) // 2, s % 2
    z, x = u // NX, u % NX
    j = k * 32 + u

    def device(zz, xx, kk):
        return (h, yh * NJ + (zz * NX + xx) * 2 + kk)

    def zat(d):
        return (z + d + NZ) % NZ

    def xat(d):
        return (x + d + NX) % NX

    def remote(src, dst, ssem, rsem, dev):
        return pltpu.make_async_remote_copy(
            src_ref=src, dst_ref=dst, send_sem=ssem, recv_sem=rsem, device_id=dev, device_id_type=MESH
        )

    plane = [(xat(d), kk) for d in (2, 1, -1, 0) for kk in (1 - k, k)][:-1]
    ring_y = [(h, (1 - yh) * NJ + s % NJ), (1 - h, s), (1 - h, (1 - yh) * NJ + s % NJ)]
    barrier = pltpu.get_barrier_semaphore()
    for dev in [device(zat(d), x, k) for d in OFF_Z] + [device(z, *p) for p in plane] + ring_y:
        pl.semaphore_signal(barrier, inc=1, device_id=dev, device_id_type=MESH)
    loads = [
        pltpu.make_async_copy(a, b, load.at[i])
        for i, (a, b) in enumerate(((rec_hbm, rec_ref), (hi_hbm, hi_ref), (lo_hbm, lo_ref), (idx_hbm, idx_ref)))
    ]
    for c in loads:
        c.start()
    for c in loads:
        c.wait()
    whiten(rec_ref, hi_ref, lo_ref, w_ref)
    pl.semaphore_wait(barrier, 17)

    def rows(kk, zz, n):
        return pl.ds(pl.multiple_of((kk * 32 + zz * NX) * 8, 8), n)

    for d in OFF_Z:
        for kk in range(2):
            remote(
                w_ref.at[rows(kk, zat(d), 32)], z_ref.at[kk, z], z_send, z_recv.at[kk, z], device(zat(d), x, k)
            ).start()
    wo = remote(w_ref, wo_ref, wo_send, wo_recv, ring_y[1])
    wo.start()
    for kk in range(2):
        z_ref[kk, z] = w_ref[rows(kk, z, 32), :]
    receivers_first(w_ref, mid_ref, 0)
    for d in (0,) + OFF_Z:
        zs = zat(d)
        if d:
            for kk in range(2):
                remote(z_ref.at[kk, zs], z_ref.at[kk, zs], z_send, z_recv.at[kk, zs], ring_y[0]).wait_recv()
        mine = k * 32 + zs * NX + x
        for xx, kk in plane:
            src = z_ref.at[kk, zs, pl.ds(pl.multiple_of(xx * 8, 8), 8)]
            remote(src, a_ref.at[mine], a_send, a_recv, device(z, xx, kk)).start()
        a_ref[mine] = z_ref[k, zs, pl.ds(pl.multiple_of(x * 8, 8), 8), :]
    wo.wait()
    receivers_first(wo_ref, mid_ref, 1)
    receivers_last(mid_ref, lhs_ref)
    some_a = remote(a_ref.at[pl.ds(0, 56)], a_ref.at[pl.ds(0, 56)], a_send, a_recv, ring_y[0])
    some_a.wait_recv()

    lane_c = lax.broadcasted_iota(jnp.int32, (8, 128), 1) & 15

    row = lax.broadcasted_iota(jnp.int32, (8, 128), 0)
    fold = jnp.where((lax.broadcasted_iota(jnp.int32, (8, 128), 1) >> 4) == row, 1.0, 0.0).astype(BF)
    trades = [
        remote(pick_ref.at[1], y_ref.at[0], y_send.at[0], y_recv.at[0], ring_y[0]),
        remote(pick_ref.at[0], y_ref.at[1], y_send.at[1], y_recv.at[1], ring_y[1]),
        remote(pick_ref.at[0], y_ref.at[2], y_send.at[2], y_recv.at[2], ring_y[2]),
    ]
    for own in range(2):
        base = (h if own else 1 - h) * 128

        def pick(i, carry):
            q = idx_ref[base + (i & 15) * 8 + (i >> 4)]
            p = q >> 4
            c = jnp.where((p >> 6) == yh, q & 15, 99)
            v = jnp.where(lane_c == c, a_ref[(p & 1) * 32 + ((p & 63) >> 1)], 0.0)
            gm_ref[own, pl.ds(pl.multiple_of(8 * i, 8), 8), :] = v
            return carry

        lax.fori_loop(0, 128, pick, 0, unroll=16)
        got = []
        for t in range(8):
            v = gm_ref[own, 128 * t : 128 * (t + 1), :]
            hi = v.astype(BF)
            rest = v - hi.astype(F32)
            mid = rest.astype(BF)
            lo = (rest - mid.astype(F32)).astype(BF)
            got.append(dot(fold, hi, 1, 1) + dot(fold, mid, 1, 1) + dot(fold, lo, 1, 1))
        for bit in range(3):
            got = swap(got, bit, lax.broadcasted_iota(jnp.int32, (8, 128), 1))
        for e in range(8):
            pick_ref[own, 8 * e : 8 * (e + 1), :] = got[e]
        if own:
            trades[0].start()
        else:
            trades[2].start()
            trades[1].start()
    for t in trades:
        t.wait()
    own = pick_ref[1] + y_ref[0]
    other = y_ref[1] + y_ref[2]
    for f2 in range(2):
        g_ref[j, f2, 0] = own[32 * f2 : 32 * f2 + 32]
        g_ref[j, f2, 1] = other[32 * f2 : 32 * f2 + 32]

    sign = 1 - 2 * k

    def source(dz, dx):
        return zat(-sign * dz) * NX + xat(-sign * dx)

    def pass_on(u2, f2, targets, over_y=False):
        blk = g_ref.at[k * 32 + u2, f2]
        devices = [device(zat(sign * dz), xat(sign * dx), k) for dz, dx in targets] + [device(z, x, 1 - k)]
        if over_y:
            devices.append(ring_y[0])
        for dev in devices:
            remote(blk, blk, g_send, g_recv.at[k * 32 + u2, f2], dev).start()

    def arrived(kk, u2, f2):
        blk = g_ref.at[kk * 32 + u2, f2]
        remote(blk, blk, g_send, g_recv.at[kk * 32 + u2, f2], ring_y[0]).wait_recv()

    def cross(*us):
        for u2 in us:
            for f2 in range(2):
                arrived(1 - k, u2, f2)
        for u2 in us:
            blocks = []
            for f2 in range(2):
                blocks += [g_ref[u2, f2].reshape(64, 128), g_ref[32 + u2, f2].reshape(64, 128)]
            hi, lo = split(jnp.concatenate(blocks, axis=0))
            res = dot(lhs_ref[u2], jnp.concatenate((hi, lo), axis=1), 1, 0)
            res = res[:128, :128] + (res[:128, 128:] + res[128:, :128])
            at = pl.ds(pl.multiple_of(8 * u2, 8), 8)
            for c in range(16):
                x_ref[c, at, :] = res[8 * c : 8 * c + 8]

    ready = []
    for tree in range(2):
        pass_on(u, (tree + yh) % 2, FIRST[tree])
    for tree, dz, dx, targets, over_y in GATHER:
        u2, f2 = source(dz, dx), (tree + yh) % 2
        if targets is None:
            ready.append(u2)
            if len(ready) == 4:
                cross(*ready)
                ready = []
        else:
            arrived(k, u2, f2)
            pass_on(u2, f2, targets, over_y)
    most_g = g_ref.at[pl.ds(0, NJ - 1)]
    remote(most_g, most_g, g_send, a_recv, ring_y[0]).wait_send()
    some_a.wait_send()
    sent_z = w_ref.at[pl.ds(0, 448)]
    remote(sent_z, sent_z, z_send, a_recv, ring_y[0]).wait_send()


def output_kernel(x_ref, hi_hbm, lo_hbm, out_ref, hi_ref, lo_ref, mix_ref, stage_ref, load, sem):
    loads = [
        pltpu.make_async_copy(hi_hbm, hi_ref, load.at[0]),
        pltpu.make_async_copy(lo_hbm, lo_ref, load.at[1]),
    ]
    for c in loads:
        c.start()
    for c in range(16):
        t = x_ref[c].T
        for half in range(2):
            mix_ref[half, pl.ds(c, 128, stride=16), :] = t[:, 128 * half : 128 * half + 128]
    copies = []
    for m in range(8):
        parts = [split(mix_ref[half, 256 * m : 256 * m + 256, :]) for half in range(2)]
        hi = jnp.concatenate([p[0] for p in parts], axis=1)
        lo = jnp.concatenate([p[1] for p in parts], axis=1)
        if m == 0:
            for c in loads:
                c.wait()
        both = dot(jnp.concatenate((hi, lo), axis=0), hi_ref[...], 1, 0)
        stage_ref[m] = both[:256] + (both[256:] + dot(hi, lo_ref[...], 1, 0))
        copy = pltpu.make_async_copy(stage_ref.at[m], out_ref.at[pl.ds(256 * m, 256)], sem.at[m])
        copy.start()
        copies.append(copy)
    for copy in copies:
        copy.wait()


def body(recording, source_channels):
    fwd_hi, fwd_lo = (jnp.asarray(t) for t in split_np(forward_table()))
    inv_hi, inv_lo = (jnp.asarray(t) for t in split_np(inverse_table()))
    dma = pltpu.SemaphoreType.DMA
    cross = pl.pallas_call(
        exchange_kernel,
        out_shape=pltpu.VMEM((16, 256, 128), F32),
        in_specs=[HBM] * 4,
        out_specs=VMEM,
        scratch_shapes=[
            pltpu.SMEM((256,), jnp.int32),
            pltpu.VMEM((256, L), F32),
            pltpu.VMEM((256, L), BF),
            pltpu.VMEM((256, L), BF),
            pltpu.VMEM((512, 128), F32),
            pltpu.VMEM((512, 128), F32),
            pltpu.VMEM((2, NZ, 32, 128), F32),
            pltpu.VMEM((NJ, 8, 128), F32),
            pltpu.VMEM((2, 1024, 128), F32),
            pltpu.VMEM((2, 64, 128), F32),
            pltpu.VMEM((3, 64, 128), F32),
            pltpu.VMEM((NJ, 2, 2, 32, 128), F32),
            pltpu.VMEM((2, 32, 16, 128), F32),
            pltpu.VMEM((32, 256, 256), BF),
            dma((4,)), dma, dma((2, NZ)), dma, dma, dma((3,)), dma((3,)), dma, dma, dma, dma((NJ, 2)),
        ],
        compiler_params=pltpu.CompilerParams(collective_id=0, has_side_effects=True),
        name="exchange",
    )(source_channels, recording.reshape(256, L), fwd_hi, fwd_lo)
    out = pl.pallas_call(
        output_kernel,
        out_shape=jax.ShapeDtypeStruct((2048, LAGS), F32),
        in_specs=[VMEM, ANY, ANY],
        out_specs=ANY,
        scratch_shapes=[
            pltpu.VMEM((256, LAGS), BF),
            pltpu.VMEM((256, LAGS), BF),
            pltpu.VMEM((2, 2048, 128), F32),
            pltpu.VMEM((8, 256, LAGS), F32),
            dma((2,)),
            dma((8,)),
        ],
        compiler_params=pltpu.CompilerParams(vmem_limit_bytes=24 << 20),
        name="correlate",
    )(cross, inv_hi, inv_lo)
    return out.reshape(128, 16, LAGS)


def solution(mesh):
    return jax.shard_map(
        body,
        mesh=mesh,
        in_specs=(P("half", "shard", None), P()),
        out_specs=P("half", "shard", None),
        check_vma=False,
    )
```

```python
import functools

import jax
import jax.numpy as jnp
import numpy as np
from jax import lax
from jax.experimental import pallas as pl
from jax.experimental.pallas import tpu as pltpu
from jax.sharding import PartitionSpec as P

F = 128
L = 1024
LAGS = 512
SEG = 32
water_level = 0.2
epsilon = 1e-05

NX, NZ = 4, 8
NJ = 64
ANY = pl.BlockSpec(memory_space=pl.ANY)
VMEM = pl.BlockSpec(memory_space=pltpu.VMEM)
HBM = pl.BlockSpec(memory_space=pltpu.HBM)
MESH = pl.DeviceIdType.MESH
BF = jnp.bfloat16
F32 = jnp.float32


def split_np(table):
    hi = table.astype(np.float32).astype(jnp.bfloat16)
    lo = (table - hi.astype(np.float64)).astype(np.float32).astype(jnp.bfloat16)
    return hi, lo


def forward_table():
    bins = np.arange(F) + 1
    times = np.arange(L)
    angle = 2.0 * np.pi * (bins[:, None] * times[None, :] % L) / L
    taper = 0.5 - 0.5 * np.cos(2.0 * np.pi * times / L)
    return np.concatenate((np.cos(angle) * taper, -np.sin(angle) * taper), axis=0)


def inverse_table():
    bins = np.arange(F) + 1
    shifts = np.arange(LAGS) - LAGS // 2
    angle = 2.0 * np.pi * (bins[:, None] * shifts[None, :] % L) / L
    table = np.stack((np.cos(angle), -np.sin(angle)), axis=1) / np.sqrt(SEG * F)
    return table.reshape(2, 32, 2, 2, LAGS).transpose(1, 2, 0, 3, 4).reshape(2 * F, LAGS)


def split(v):
    hi = v.astype(BF)
    return hi, (v - hi.astype(F32)).astype(BF)


def dot(a, b, ca, cb):
    return lax.dot_general(a, b, (((ca,), (cb,)), ((), ())), preferred_element_type=F32)


OFF_Z = (4, 3, -3, 2, -2, 1, -1)
FIRST = (
    ((-1, 0), (2, 0), (0, -2), (4, 0)),
    ((0, 1), (0, -1), (2, 0)),
)
GATHER = (
    (0, 0, 0, None, 0), (0, -1, 0, ((0, 1), (-1, 0), (0, -1)), 1), (1, 0, 1, ((-3, 0), (1, 0)), 0),
    (1, 0, -1, ((0, -1),), 0), (0, 0, 2, ((1, 0), (0, 1)), 0), (0, 2, 0, ((0, -2), (0, 1), (0, -1)), 0),
    (1, 2, 0, ((1, 0),), 0), (0, -1, 1, ((0, 1), (1, 0)), 0), (0, -2, 0, ((-1, 0), (0, 1)), 1),
    (0, -1, -1, ((-1, 0),), 0), (1, 0, 2, ((-1, 0),), 0), (1, -1, 0, (), 0), (1, 1, 1, ((1, 0), (0, -1)), 0),
    (0, 0, -1, (), 0), (0, 4, 0, ((0, 1), (0, -1)), 1), (0, 0, 2, None, 0), (0, 2, 1, ((1, 0),), 0),
    (0, 1, 2, ((0, 1), (0, -1)), 1), (0, 2, -1, (), 1), (1, 3, 0, ((0, -1), (0, 1)), 0),
    (0, 2, 2, ((1, 0), (2, 0)), 1), (1, -3, 1, ((0, 1), (1, 0), (0, -1)), 0), (0, -1, 2, ((-1, 0),), 0),
    (0, 0, 1, (), 0), (0, 0, 1, None, 0), (0, -2, 1, (), 0), (0, -2, -1, (), 1), (1, 1, 0, (), 0), (1, -2, 0, (), 0),
    (0, -3, 0, ((-2, 0), (0, -1)), 0), (0, 4, 1, ((1, 0),), 0), (1, -1, 2, ((0, -1), (0, 1)), 0), (0, 0, -1, None, 0),
    (0, 4, -1, ((-1, 0),), 1), (1, 2, 1, ((2, 0),), 0), (1, 4, 0, (), 0), (0, 1, -1, ((0, 1),), 1), (0, 3, 1, (), 0),
    (0, 1, 1, (), 0), (0, 3, 2, (), 0), (1, 1, 2, (), 0), (0, 1, 2, None, 0), (1, 3, -1, ((0, -1),), 0),
    (1, 3, 1, (), 0), (1, -2, 1, ((0, 1),), 0), (1, 2, -1, (), 0), (1, -3, 2, ((0, 1), (-1, 0)), 0),
    (0, -2, 2, ((-1, 0),), 0), (1, -3, 0, (), 0), (0, 4, 2, (), 0), (1, 2, 2, (), 0), (0, -3, -1, (), 0),
    (1, -1, 1, (), 0), (0, 2, 0, None, 0), (0, 4, 0, None, 0), (0, 2, -1, None, 0), (1, -2, -1, (), 0),
    (1, -1, -1, (), 0), (0, -1, -1, None, 0), (0, -3, 1, (), 0), (0, 1, 0, (), 0), (0, -1, 2, None, 0),
    (0, 1, 0, None, 0), (0, -2, 1, None, 0), (0, 3, -1, (), 0), (1, 4, -1, (), 0), (0, 3, 0, (), 0), (1, 3, 2, (), 0),
    (0, 3, 0, None, 0), (1, 4, 1, (), 0), (1, -2, 2, (), 0), (0, 1, 1, None, 0), (1, 1, -1, (), 0),
    (1, -3, -1, (), 0), (1, 4, 2, (), 0), (0, -3, -1, None, 0), (0, -3, 2, (), 0), (0, -3, 1, None, 0),
    (0, 3, -1, None, 0), (0, -2, 2, None, 0), (0, -1, 0, None, 0), (0, -3, 0, None, 0), (0, -3, 2, None, 0),
    (0, 4, -1, None, 0), (0, 2, 1, None, 0), (0, 4, 1, None, 0), (0, 2, 2, None, 0), (0, 3, 1, None, 0),
    (0, 4, 2, None, 0), (0, -1, 1, None, 0), (0, 3, 2, None, 0), (0, -2, 0, None, 0), (0, -2, -1, None, 0),
    (0, 1, -1, None, 0),
)


def whiten(rec_ref, hi_ref, lo_ref, out_ref):
    rec_hi, rec_lo = split(rec_ref[...])
    spec = dot(hi_ref[...], rec_hi, 1, 1) + dot(hi_ref[...], rec_lo, 1, 1) + dot(lo_ref[...], rec_hi, 1, 1)
    re, im = spec[:F], spec[F:]
    mag = jnp.sqrt(re * re + im * im)
    zeros = jnp.zeros((2, mag.shape[1]), F32)
    pad = jnp.concatenate((zeros, mag, zeros), axis=0)
    smooth = pad[0:F]
    for off in range(1, 5):
        smooth = smooth + pad[off : off + F]
    mean = jnp.sum(mag, axis=0, keepdims=True) * (1.0 / F)
    divisor = smooth / 5.0 + water_level * mean + epsilon
    for q, part in enumerate((re, im)):
        white = part / divisor
        for s_hi in range(2):
            out_ref[pl.ds(2 * q + s_hi, F, stride=4), :] = white[:, 128 * s_hi : 128 * (s_hi + 1)]


def swap(v, bit, lane):
    step = 1 << bit
    low = (lane & step) == 0
    v = list(v)
    for i in range(len(v)):
        if i & step:
            continue
        a, b = v[i], v[i + step]
        v[i] = jnp.where(low, a, pltpu.roll(b, step, 1))
        v[i + step] = jnp.where(low, pltpu.roll(a, 128 - step, 1), b)
    return v


def lanes():
    return lax.broadcasted_iota(jnp.int32, (16, 128), 1)


def receivers_first(ref, mid_ref, side):
    v = []
    for e in range(4):
        t = ref[pl.ds(e, F, stride=4), :].T
        v += [t[16 * i : 16 * i + 16] for i in range(8)]
    for bit in range(5):
        v = swap(v, bit, lanes())
    for i in range(32):
        mid_ref[side, i] = v[i]


def receivers_last(mid_ref, lhs_ref):
    lane = lanes()
    first = (lane & 16) == 0
    low = (lane & 32) == 0
    row8 = lax.broadcasted_iota(jnp.int32, (8, 128), 0)
    lane8 = lax.broadcasted_iota(jnp.int32, (8, 128), 1)
    imag = (row8 & 1) == 1
    same = ((row8 >> 1) & 1) == (lane8 >> 6)
    keep = [same & ((row8 >> 2) == f2) for f2 in range(2)]
    for i in range(32):
        a, b = mid_ref[0, i], mid_ref[1, i]
        pair = (jnp.where(low, a, pltpu.roll(b, 32, 1)), jnp.where(low, pltpu.roll(a, 96, 1), b))
        for half in range(2):
            g = 32 * half + i
            u, f2 = g // 2, g % 2
            re = pair[half]
            im = jnp.where(first, pltpu.roll(re, 112, 1), -pltpu.roll(re, 16, 1))
            rows = []
            for c in range(16):
                v = jnp.where(
                    imag, jnp.broadcast_to(im[c : c + 1], (8, 128)), jnp.broadcast_to(re[c : c + 1], (8, 128))
                )
                rows.append(jnp.where(keep[f2], v, 0.0))
            hi, lo = split(jnp.concatenate(rows, axis=0))
            lhs_ref[u, 0:128, 128 * f2 : 128 * f2 + 128] = hi
            lhs_ref[u, 128:256, 128 * f2 : 128 * f2 + 128] = lo


def exchange_kernel(idx_hbm, rec_hbm, hi_hbm, lo_hbm, x_ref, idx_ref, rec_ref, hi_ref, lo_ref, w_ref, wo_ref, z_ref, a_ref,
                    gm_ref, pick_ref, y_ref, g_ref, mid_ref, lhs_ref,
                    load, z_send, z_recv, a_send, a_recv, y_send, y_recv, wo_send, wo_recv, g_send, g_recv):
    h = lax.axis_index("half")
    s = lax.axis_index("shard")
    yh, u, k = s // NJ, (s % NJ) // 2, s % 2
    z, x = u // NX, u % NX
    j = k * 32 + u

    def device(zz, xx, kk):
        return (h, yh * NJ + (zz * NX + xx) * 2 + kk)

    def zat(d):
        return (z + d + NZ) % NZ

    def xat(d):
        return (x + d + NX) % NX

    def remote(src, dst, ssem, rsem, dev):
        return pltpu.make_async_remote_copy(
            src_ref=src, dst_ref=dst, send_sem=ssem, recv_sem=rsem, device_id=dev, device_id_type=MESH
        )

    plane = [(xat(d), kk) for d in (2, 1, -1, 0) for kk in (1 - k, k)][:-1]
    ring_y = [(h, (1 - yh) * NJ + s % NJ), (1 - h, s), (1 - h, (1 - yh) * NJ + s % NJ)]
    barrier = pltpu.get_barrier_semaphore()
    for dev in [device(zat(d), x, k) for d in OFF_Z] + [device(z, *p) for p in plane] + ring_y:
        pl.semaphore_signal(barrier, inc=1, device_id=dev, device_id_type=MESH)
    loads = [
        pltpu.make_async_copy(a, b, load.at[i])
        for i, (a, b) in enumerate(((rec_hbm, rec_ref), (hi_hbm, hi_ref), (lo_hbm, lo_ref), (idx_hbm, idx_ref)))
    ]
    for c in loads:
        c.start()
    for c in loads:
        c.wait()
    whiten(rec_ref, hi_ref, lo_ref, w_ref)
    pl.semaphore_wait(barrier, 17)

    def rows(kk, zz, n):
        return pl.ds(pl.multiple_of((kk * 32 + zz * NX) * 8, 8), n)

    for d in OFF_Z:
        for kk in range(2):
            remote(
                w_ref.at[rows(kk, zat(d), 32)], z_ref.at[kk, z], z_send, z_recv.at[kk, z], device(zat(d), x, k)
            ).start()
    wo = remote(w_ref, wo_ref, wo_send, wo_recv, ring_y[1])
    wo.start()
    for kk in range(2):
        z_ref[kk, z] = w_ref[rows(kk, z, 32), :]
    receivers_first(w_ref, mid_ref, 0)
    for d in (0,) + OFF_Z:
        zs = zat(d)
        if d:
            for kk in range(2):
                remote(z_ref.at[kk, zs], z_ref.at[kk, zs], z_send, z_recv.at[kk, zs], ring_y[0]).wait_recv()
        mine = k * 32 + zs * NX + x
        for xx, kk in plane:
            src = z_ref.at[kk, zs, pl.ds(pl.multiple_of(xx * 8, 8), 8)]
            remote(src, a_ref.at[mine], a_send, a_recv, device(z, xx, kk)).start()
        a_ref[mine] = z_ref[k, zs, pl.ds(pl.multiple_of(x * 8, 8), 8), :]
    wo.wait()
    receivers_first(wo_ref, mid_ref, 1)
    receivers_last(mid_ref, lhs_ref)
    some_a = remote(a_ref.at[pl.ds(0, 56)], a_ref.at[pl.ds(0, 56)], a_send, a_recv, ring_y[0])
    some_a.wait_recv()

    lane_c = lax.broadcasted_iota(jnp.int32, (8, 128), 1) & 15

    row = lax.broadcasted_iota(jnp.int32, (8, 128), 0)
    fold = jnp.where((lax.broadcasted_iota(jnp.int32, (8, 128), 1) >> 4) == row, 1.0, 0.0).astype(BF)
    trades = [
        remote(pick_ref.at[1], y_ref.at[0], y_send.at[0], y_recv.at[0], ring_y[0]),
        remote(pick_ref.at[0], y_ref.at[1], y_send.at[1], y_recv.at[1], ring_y[1]),
        remote(pick_ref.at[0], y_ref.at[2], y_send.at[2], y_recv.at[2], ring_y[2]),
    ]
    for own in (1, 0):
        base = (h if own else 1 - h) * 128

        def pick(i, carry):
            q = idx_ref[base + (i & 15) * 8 + (i >> 4)]
            p = q >> 4
            c = jnp.where((p >> 6) == yh, q & 15, 99)
            v = jnp.where(lane_c == c, a_ref[(p & 1) * 32 + ((p & 63) >> 1)], 0.0)
            gm_ref[own, pl.ds(pl.multiple_of(8 * i, 8), 8), :] = v
            return carry

        lax.fori_loop(0, 128, pick, 0, unroll=16)
        got = []
        for t in range(8):
            v = gm_ref[own, 128 * t : 128 * (t + 1), :]
            hi = v.astype(BF)
            rest = v - hi.astype(F32)
            mid = rest.astype(BF)
            lo = (rest - mid.astype(F32)).astype(BF)
            got.append(dot(fold, hi, 1, 1) + dot(fold, mid, 1, 1) + dot(fold, lo, 1, 1))
        for bit in range(3):
            got = swap(got, bit, lax.broadcasted_iota(jnp.int32, (8, 128), 1))
        for e in range(8):
            pick_ref[own, 8 * e : 8 * (e + 1), :] = got[e]
        if own:
            trades[0].start()
        else:
            trades[2].start()
            trades[1].start()
    for t in trades:
        t.wait()
    own = pick_ref[1] + y_ref[0]
    other = y_ref[1] + y_ref[2]
    for f2 in range(2):
        g_ref[j, f2, 0] = own[32 * f2 : 32 * f2 + 32]
        g_ref[j, f2, 1] = other[32 * f2 : 32 * f2 + 32]

    sign = 1 - 2 * k

    def source(dz, dx):
        return zat(-sign * dz) * NX + xat(-sign * dx)

    def pass_on(u2, f2, targets, over_y=False):
        blk = g_ref.at[k * 32 + u2, f2]
        devices = [device(zat(sign * dz), xat(sign * dx), k) for dz, dx in targets] + [device(z, x, 1 - k)]
        if over_y:
            devices.append(ring_y[0])
        for dev in devices:
            remote(blk, blk, g_send, g_recv.at[k * 32 + u2, f2], dev).start()

    def arrived(kk, u2, f2):
        blk = g_ref.at[kk * 32 + u2, f2]
        remote(blk, blk, g_send, g_recv.at[kk * 32 + u2, f2], ring_y[0]).wait_recv()

    def cross(*us):
        for u2 in us:
            for f2 in range(2):
                arrived(1 - k, u2, f2)
        for u2 in us:
            blocks = []
            for f2 in range(2):
                blocks += [g_ref[u2, f2].reshape(64, 128), g_ref[32 + u2, f2].reshape(64, 128)]
            hi, lo = split(jnp.concatenate(blocks, axis=0))
            res = dot(lhs_ref[u2], jnp.concatenate((hi, lo), axis=1), 1, 0)
            res = res[:128, :128] + (res[:128, 128:] + res[128:, :128])
            at = pl.ds(pl.multiple_of(8 * u2, 8), 8)
            for c in range(16):
                x_ref[c, at, :] = res[8 * c : 8 * c + 8]

    ready = []
    for tree in range(2):
        pass_on(u, (tree + yh) % 2, FIRST[tree])
    for tree, dz, dx, targets, over_y in GATHER:
        u2, f2 = source(dz, dx), (tree + yh) % 2
        if targets is None:
            ready.append(u2)
            if len(ready) == 4:
                cross(*ready)
                ready = []
        else:
            arrived(k, u2, f2)
            pass_on(u2, f2, targets, over_y)
    most_g = g_ref.at[pl.ds(0, NJ - 1)]
    remote(most_g, most_g, g_send, a_recv, ring_y[0]).wait_send()
    some_a.wait_send()
    sent_z = w_ref.at[pl.ds(0, 448)]
    remote(sent_z, sent_z, z_send, a_recv, ring_y[0]).wait_send()


def output_kernel(x_ref, hi_hbm, lo_hbm, out_ref, hi_ref, lo_ref, mix_ref, stage_ref, load, sem):
    loads = [
        pltpu.make_async_copy(hi_hbm, hi_ref, load.at[0]),
        pltpu.make_async_copy(lo_hbm, lo_ref, load.at[1]),
    ]
    for c in loads:
        c.start()
    for c in range(16):
        t = x_ref[c].T
        for half in range(2):
            mix_ref[half, pl.ds(c, 128, stride=16), :] = t[:, 128 * half : 128 * half + 128]
    copies = []
    for m in range(8):
        parts = [split(mix_ref[half, 256 * m : 256 * m + 256, :]) for half in range(2)]
        hi = jnp.concatenate([p[0] for p in parts], axis=1)
        lo = jnp.concatenate([p[1] for p in parts], axis=1)
        if m == 0:
            for c in loads:
                c.wait()
        both = dot(jnp.concatenate((hi, lo), axis=0), hi_ref[...], 1, 0)
        stage_ref[m] = both[:256] + (both[256:] + dot(hi, lo_ref[...], 1, 0))
        copy = pltpu.make_async_copy(stage_ref.at[m], out_ref.at[pl.ds(256 * m, 256)], sem.at[m])
        copy.start()
        copies.append(copy)
    for copy in copies:
        copy.wait()


def body(recording, source_channels):
    fwd_hi, fwd_lo = (jnp.asarray(t) for t in split_np(forward_table()))
    inv_hi, inv_lo = (jnp.asarray(t) for t in split_np(inverse_table()))
    dma = pltpu.SemaphoreType.DMA
    cross = pl.pallas_call(
        exchange_kernel,
        out_shape=pltpu.VMEM((16, 256, 128), F32),
        in_specs=[HBM] * 4,
        out_specs=VMEM,
        scratch_shapes=[
            pltpu.SMEM((256,), jnp.int32),
            pltpu.VMEM((256, L), F32),
            pltpu.VMEM((256, L), BF),
            pltpu.VMEM((256, L), BF),
            pltpu.VMEM((512, 128), F32),
            pltpu.VMEM((512, 128), F32),
            pltpu.VMEM((2, NZ, 32, 128), F32),
            pltpu.VMEM((NJ, 8, 128), F32),
            pltpu.VMEM((2, 1024, 128), F32),
            pltpu.VMEM((2, 64, 128), F32),
            pltpu.VMEM((3, 64, 128), F32),
            pltpu.VMEM((NJ, 2, 2, 32, 128), F32),
            pltpu.VMEM((2, 32, 16, 128), F32),
            pltpu.VMEM((32, 256, 256), BF),
            dma((4,)), dma, dma((2, NZ)), dma, dma, dma((3,)), dma((3,)), dma, dma, dma, dma((NJ, 2)),
        ],
        compiler_params=pltpu.CompilerParams(collective_id=0, has_side_effects=True),
        name="exchange",
    )(source_channels, recording.reshape(256, L), fwd_hi, fwd_lo)
    out = pl.pallas_call(
        output_kernel,
        out_shape=jax.ShapeDtypeStruct((2048, LAGS), F32),
        in_specs=[VMEM, ANY, ANY],
        out_specs=ANY,
        scratch_shapes=[
            pltpu.VMEM((256, LAGS), BF),
            pltpu.VMEM((256, LAGS), BF),
            pltpu.VMEM((2, 2048, 128), F32),
            pltpu.VMEM((8, 256, LAGS), F32),
            dma((2,)),
            dma((8,)),
        ],
        compiler_params=pltpu.CompilerParams(vmem_limit_bytes=24 << 20),
        name="correlate",
    )(cross, inv_hi, inv_lo)
    return out.reshape(128, 16, LAGS)


def solution(mesh):
    return jax.shard_map(
        body,
        mesh=mesh,
        in_specs=(P("half", "shard", None), P()),
        out_specs=P("half", "shard", None),
        check_vma=False,
    )
```

```python
import functools

import jax
import jax.numpy as jnp
import numpy as np
from jax import lax
from jax.experimental import pallas as pl
from jax.experimental.pallas import tpu as pltpu
from jax.sharding import PartitionSpec as P

F = 128
L = 1024
LAGS = 512
SEG = 32
water_level = 0.2
epsilon = 1e-05

NX, NZ = 4, 8
NJ = 64
ANY = pl.BlockSpec(memory_space=pl.ANY)
VMEM = pl.BlockSpec(memory_space=pltpu.VMEM)
HBM = pl.BlockSpec(memory_space=pltpu.HBM)
MESH = pl.DeviceIdType.MESH
BF = jnp.bfloat16
F32 = jnp.float32


def split_np(table):
    hi = table.astype(np.float32).astype(jnp.bfloat16)
    lo = (table - hi.astype(np.float64)).astype(np.float32).astype(jnp.bfloat16)
    return hi, lo


def forward_table():
    bins = np.arange(F) + 1
    times = np.arange(L)
    angle = 2.0 * np.pi * (bins[:, None] * times[None, :] % L) / L
    taper = 0.5 - 0.5 * np.cos(2.0 * np.pi * times / L)
    return np.concatenate((np.cos(angle) * taper, -np.sin(angle) * taper), axis=0)


def inverse_table():
    bins = np.arange(F) + 1
    shifts = np.arange(LAGS) - LAGS // 2
    angle = 2.0 * np.pi * (bins[:, None] * shifts[None, :] % L) / L
    table = np.stack((np.cos(angle), -np.sin(angle)), axis=1) / np.sqrt(SEG * F)
    return table.reshape(2, 32, 2, 2, LAGS).transpose(1, 2, 0, 3, 4).reshape(2 * F, LAGS)


def split(v):
    hi = v.astype(BF)
    return hi, (v - hi.astype(F32)).astype(BF)


def dot(a, b, ca, cb):
    return lax.dot_general(a, b, (((ca,), (cb,)), ((), ())), preferred_element_type=F32)


OFF_Z = (4, 3, -3, 2, -2, 1, -1)
FIRST = (
    ((-1, 0), (2, 0), (0, -2), (4, 0)),
    ((0, 1), (0, -1), (2, 0)),
)
GATHER = (
    (0, 0, 0, None, 0), (0, -1, 0, ((0, 1), (-1, 0), (0, -1)), 1), (1, 0, 1, ((-3, 0), (1, 0)), 0),
    (1, 0, -1, ((0, -1),), 0), (0, 0, 2, ((1, 0), (0, 1)), 0), (0, 2, 0, ((0, -2), (0, 1), (0, -1)), 0),
    (1, 2, 0, ((1, 0),), 0), (0, -1, 1, ((0, 1), (1, 0)), 0), (0, -2, 0, ((-1, 0), (0, 1)), 1),
    (0, -1, -1, ((-1, 0),), 0), (1, 0, 2, ((-1, 0),), 0), (1, -1, 0, (), 0), (1, 1, 1, ((1, 0), (0, -1)), 0),
    (0, 0, -1, (), 0), (0, 4, 0, ((0, 1), (0, -1)), 1), (0, 0, 2, None, 0), (0, 2, 1, ((1, 0),), 0),
    (0, 1, 2, ((0, 1), (0, -1)), 1), (0, 2, -1, (), 1), (1, 3, 0, ((0, -1), (0, 1)), 0),
    (0, 2, 2, ((1, 0), (2, 0)), 1), (1, -3, 1, ((0, 1), (1, 0), (0, -1)), 0), (0, -1, 2, ((-1, 0),), 0),
    (0, 0, 1, (), 0), (0, 0, 1, None, 0), (0, -2, 1, (), 0), (0, -2, -1, (), 1), (1, 1, 0, (), 0), (1, -2, 0, (), 0),
    (0, -3, 0, ((-2, 0), (0, -1)), 0), (0, 4, 1, ((1, 0),), 0), (1, -1, 2, ((0, -1), (0, 1)), 0), (0, 0, -1, None, 0),
    (0, 4, -1, ((-1, 0),), 1), (1, 2, 1, ((2, 0),), 0), (1, 4, 0, (), 0), (0, 1, -1, ((0, 1),), 1), (0, 3, 1, (), 0),
    (0, 1, 1, (), 0), (0, 3, 2, (), 0), (1, 1, 2, (), 0), (0, 1, 2, None, 0), (1, 3, -1, ((0, -1),), 0),
    (1, 3, 1, (), 0), (1, -2, 1, ((0, 1),), 0), (1, 2, -1, (), 0), (1, -3, 2, ((0, 1), (-1, 0)), 0),
    (0, -2, 2, ((-1, 0),), 0), (1, -3, 0, (), 0), (0, 4, 2, (), 0), (1, 2, 2, (), 0), (0, -3, -1, (), 0),
    (1, -1, 1, (), 0), (0, 2, 0, None, 0), (0, 4, 0, None, 0), (0, 2, -1, None, 0), (1, -2, -1, (), 0),
    (1, -1, -1, (), 0), (0, -1, -1, None, 0), (0, -3, 1, (), 0), (0, 1, 0, (), 0), (0, -1, 2, None, 0),
    (0, 1, 0, None, 0), (0, -2, 1, None, 0), (0, 3, -1, (), 0), (1, 4, -1, (), 0), (0, 3, 0, (), 0), (1, 3, 2, (), 0),
    (0, 3, 0, None, 0), (1, 4, 1, (), 0), (1, -2, 2, (), 0), (0, 1, 1, None, 0), (1, 1, -1, (), 0),
    (1, -3, -1, (), 0), (1, 4, 2, (), 0), (0, -3, -1, None, 0), (0, -3, 2, (), 0), (0, -3, 1, None, 0),
    (0, 3, -1, None, 0), (0, -2, 2, None, 0), (0, -1, 0, None, 0), (0, -3, 0, None, 0), (0, -3, 2, None, 0),
    (0, 4, -1, None, 0), (0, 2, 1, None, 0), (0, 4, 1, None, 0), (0, 2, 2, None, 0), (0, 3, 1, None, 0),
    (0, 4, 2, None, 0), (0, -1, 1, None, 0), (0, 3, 2, None, 0), (0, -2, 0, None, 0), (0, -2, -1, None, 0),
    (0, 1, -1, None, 0),
)


def whiten(rec_ref, hi_ref, lo_ref, out_ref):
    rec_hi, rec_lo = split(rec_ref[...])
    spec = dot(hi_ref[...], rec_hi, 1, 1) + dot(hi_ref[...], rec_lo, 1, 1) + dot(lo_ref[...], rec_hi, 1, 1)
    re, im = spec[:F], spec[F:]
    mag = jnp.sqrt(re * re + im * im)
    zeros = jnp.zeros((2, mag.shape[1]), F32)
    pad = jnp.concatenate((zeros, mag, zeros), axis=0)
    smooth = pad[0:F]
    for off in range(1, 5):
        smooth = smooth + pad[off : off + F]
    mean = jnp.sum(mag, axis=0, keepdims=True) * (1.0 / F)
    divisor = smooth / 5.0 + water_level * mean + epsilon
    for q, part in enumerate((re, im)):
        white = part / divisor
        for s_hi in range(2):
            out_ref[pl.ds(2 * q + s_hi, F, stride=4), :] = white[:, 128 * s_hi : 128 * (s_hi + 1)]


def swap(v, bit, lane):
    step = 1 << bit
    low = (lane & step) == 0
    v = list(v)
    for i in range(len(v)):
        if i & step:
            continue
        a, b = v[i], v[i + step]
        v[i] = jnp.where(low, a, pltpu.roll(b, step, 1))
        v[i + step] = jnp.where(low, pltpu.roll(a, 128 - step, 1), b)
    return v


def lanes():
    return lax.broadcasted_iota(jnp.int32, (16, 128), 1)


def receivers_first(ref, mid_ref, side):
    v = []
    for e in range(4):
        t = ref[pl.ds(e, F, stride=4), :].T
        v += [t[16 * i : 16 * i + 16] for i in range(8)]
    for bit in range(5):
        v = swap(v, bit, lanes())
    for i in range(32):
        mid_ref[side, i] = v[i]


def receivers_last(mid_ref, lhs_ref):
    lane = lanes()
    first = (lane & 16) == 0
    low = (lane & 32) == 0
    row8 = lax.broadcasted_iota(jnp.int32, (8, 128), 0)
    lane8 = lax.broadcasted_iota(jnp.int32, (8, 128), 1)
    imag = (row8 & 1) == 1
    same = ((row8 >> 1) & 1) == (lane8 >> 6)
    keep = [same & ((row8 >> 2) == f2) for f2 in range(2)]
    for i in range(32):
        a, b = mid_ref[0, i], mid_ref[1, i]
        pair = (jnp.where(low, a, pltpu.roll(b, 32, 1)), jnp.where(low, pltpu.roll(a, 96, 1), b))
        for half in range(2):
            g = 32 * half + i
            u, f2 = g // 2, g % 2
            re = pair[half]
            im = jnp.where(first, pltpu.roll(re, 112, 1), -pltpu.roll(re, 16, 1))
            rows = []
            for c in range(16):
                v = jnp.where(
                    imag, jnp.broadcast_to(im[c : c + 1], (8, 128)), jnp.broadcast_to(re[c : c + 1], (8, 128))
                )
                rows.append(jnp.where(keep[f2], v, 0.0))
            hi, lo = split(jnp.concatenate(rows, axis=0))
            lhs_ref[u, 0:128, 128 * f2 : 128 * f2 + 128] = hi
            lhs_ref[u, 128:256, 128 * f2 : 128 * f2 + 128] = lo


def exchange_kernel(idx_hbm, rec_hbm, hi_hbm, lo_hbm, x_ref, idx_ref, rec_ref, hi_ref, lo_ref, w_ref, wo_ref, z_ref, a_ref,
                    gm_ref, pick_ref, y_ref, g_ref, mid_ref, lhs_ref,
                    load, z_send, z_recv, a_send, a_recv, y_send, y_recv, wo_send, wo_recv, g_send, g_recv):
    h = lax.axis_index("half")
    s = lax.axis_index("shard")
    yh, u, k = s // NJ, (s % NJ) // 2, s % 2
    z, x = u // NX, u % NX
    j = k * 32 + u

    def device(zz, xx, kk):
        return (h, yh * NJ + (zz * NX + xx) * 2 + kk)

    def zat(d):
        return (z + d + NZ) % NZ

    def xat(d):
        return (x + d + NX) % NX

    def remote(src, dst, ssem, rsem, dev):
        return pltpu.make_async_remote_copy(
            src_ref=src, dst_ref=dst, send_sem=ssem, recv_sem=rsem, device_id=dev, device_id_type=MESH
        )

    plane = [(xat(d), kk) for d in (2, 1, -1, 0) for kk in (1 - k, k)][:-1]
    ring_y = [(h, (1 - yh) * NJ + s % NJ), (1 - h, s), (1 - h, (1 - yh) * NJ + s % NJ)]
    barrier = pltpu.get_barrier_semaphore()
    for dev in [device(zat(d), x, k) for d in OFF_Z] + [device(z, *p) for p in plane] + ring_y:
        pl.semaphore_signal(barrier, inc=1, device_id=dev, device_id_type=MESH)
    loads = [
        pltpu.make_async_copy(a, b, load.at[i])
        for i, (a, b) in enumerate(((rec_hbm, rec_ref), (hi_hbm, hi_ref), (lo_hbm, lo_ref), (idx_hbm, idx_ref)))
    ]
    for c in loads:
        c.start()
    for c in loads:
        c.wait()
    whiten(rec_ref, hi_ref, lo_ref, w_ref)
    pl.semaphore_wait(barrier, 17)

    def rows(kk, zz, n):
        return pl.ds(pl.multiple_of((kk * 32 + zz * NX) * 8, 8), n)

    for d in OFF_Z:
        for kk in range(2):
            remote(
                w_ref.at[rows(kk, zat(d), 32)], z_ref.at[kk, z], z_send, z_recv.at[kk, z], device(zat(d), x, k)
            ).start()
    wo = remote(w_ref, wo_ref, wo_send, wo_recv, ring_y[1])
    wo.start()
    for kk in range(2):
        z_ref[kk, z] = w_ref[rows(kk, z, 32), :]
    receivers_first(w_ref, mid_ref, 0)
    for d in (0,) + OFF_Z:
        zs = zat(d)
        if d:
            for kk in range(2):
                remote(z_ref.at[kk, zs], z_ref.at[kk, zs], z_send, z_recv.at[kk, zs], ring_y[0]).wait_recv()
        mine = k * 32 + zs * NX + x
        for xx, kk in plane:
            src = z_ref.at[kk, zs, pl.ds(pl.multiple_of(xx * 8, 8), 8)]
            remote(src, a_ref.at[mine], a_send, a_recv, device(z, xx, kk)).start()
        a_ref[mine] = z_ref[k, zs, pl.ds(pl.multiple_of(x * 8, 8), 8), :]
    wo.wait()
    receivers_first(wo_ref, mid_ref, 1)
    receivers_last(mid_ref, lhs_ref)
    some_a = remote(a_ref.at[pl.ds(0, 56)], a_ref.at[pl.ds(0, 56)], a_send, a_recv, ring_y[0])
    some_a.wait_recv()

    lane_c = lax.broadcasted_iota(jnp.int32, (8, 128), 1) & 15

    row = lax.broadcasted_iota(jnp.int32, (8, 128), 0)
    fold = jnp.where((lax.broadcasted_iota(jnp.int32, (8, 128), 1) >> 4) == row, 1.0, 0.0).astype(BF)
    trades = [
        remote(pick_ref.at[1], y_ref.at[0], y_send.at[0], y_recv.at[0], ring_y[0]),
        remote(pick_ref.at[0], y_ref.at[1], y_send.at[1], y_recv.at[1], ring_y[1]),
        remote(pick_ref.at[0], y_ref.at[2], y_send.at[2], y_recv.at[2], ring_y[2]),
    ]
    for own in (1, 0):
        base = (h if own else 1 - h) * 128

        def pick(i, carry):
            q = idx_ref[base + (i & 15) * 8 + (i >> 4)]
            p = q >> 4
            c = jnp.where((p >> 6) == yh, q & 15, 99)
            v = jnp.where(lane_c == c, a_ref[(p & 1) * 32 + ((p & 63) >> 1)], 0.0)
            gm_ref[own, pl.ds(pl.multiple_of(8 * i, 8), 8), :] = v
            return carry

        lax.fori_loop(0, 128, pick, 0, unroll=32)
        got = []
        for t in range(8):
            v = gm_ref[own, 128 * t : 128 * (t + 1), :]
            hi = v.astype(BF)
            rest = v - hi.astype(F32)
            mid = rest.astype(BF)
            lo = (rest - mid.astype(F32)).astype(BF)
            got.append(dot(fold, hi, 1, 1) + dot(fold, mid, 1, 1) + dot(fold, lo, 1, 1))
        for bit in range(3):
            got = swap(got, bit, lax.broadcasted_iota(jnp.int32, (8, 128), 1))
        for e in range(8):
            pick_ref[own, 8 * e : 8 * (e + 1), :] = got[e]
        if own:
            trades[0].start()
        else:
            trades[2].start()
            trades[1].start()
    for t in trades:
        t.wait()
    own = pick_ref[1] + y_ref[0]
    other = y_ref[1] + y_ref[2]
    for f2 in range(2):
        g_ref[j, f2, 0] = own[32 * f2 : 32 * f2 + 32]
        g_ref[j, f2, 1] = other[32 * f2 : 32 * f2 + 32]

    sign = 1 - 2 * k

    def source(dz, dx):
        return zat(-sign * dz) * NX + xat(-sign * dx)

    def pass_on(u2, f2, targets, over_y=False):
        blk = g_ref.at[k * 32 + u2, f2]
        devices = [device(zat(sign * dz), xat(sign * dx), k) for dz, dx in targets] + [device(z, x, 1 - k)]
        if over_y:
            devices.append(ring_y[0])
        for dev in devices:
            remote(blk, blk, g_send, g_recv.at[k * 32 + u2, f2], dev).start()

    def arrived(kk, u2, f2):
        blk = g_ref.at[kk * 32 + u2, f2]
        remote(blk, blk, g_send, g_recv.at[kk * 32 + u2, f2], ring_y[0]).wait_recv()

    def cross(*us):
        for u2 in us:
            for f2 in range(2):
                arrived(1 - k, u2, f2)
        for u2 in us:
            blocks = []
            for f2 in range(2):
                blocks += [g_ref[u2, f2].reshape(64, 128), g_ref[32 + u2, f2].reshape(64, 128)]
            hi, lo = split(jnp.concatenate(blocks, axis=0))
            res = dot(lhs_ref[u2], jnp.concatenate((hi, lo), axis=1), 1, 0)
            res = res[:128, :128] + (res[:128, 128:] + res[128:, :128])
            at = pl.ds(pl.multiple_of(8 * u2, 8), 8)
            for c in range(16):
                x_ref[c, at, :] = res[8 * c : 8 * c + 8]

    ready = []
    for tree in (1, 0):
        pass_on(u, (tree + yh) % 2, FIRST[tree])
    for tree, dz, dx, targets, over_y in GATHER:
        u2, f2 = source(dz, dx), (tree + yh) % 2
        if targets is None:
            ready.append(u2)
            if len(ready) == 4:
                cross(*ready)
                ready = []
        else:
            arrived(k, u2, f2)
            pass_on(u2, f2, targets, over_y)
    most_g = g_ref.at[pl.ds(0, NJ - 1)]
    remote(most_g, most_g, g_send, a_recv, ring_y[0]).wait_send()
    some_a.wait_send()
    sent_z = w_ref.at[pl.ds(0, 448)]
    remote(sent_z, sent_z, z_send, a_recv, ring_y[0]).wait_send()


def output_kernel(x_ref, hi_hbm, lo_hbm, out_ref, hi_ref, lo_ref, mix_ref, stage_ref, load, sem):
    loads = [
        pltpu.make_async_copy(hi_hbm, hi_ref, load.at[0]),
        pltpu.make_async_copy(lo_hbm, lo_ref, load.at[1]),
    ]
    for c in loads:
        c.start()
    for c in range(16):
        t = x_ref[c].T
        for half in range(2):
            mix_ref[half, pl.ds(c, 128, stride=16), :] = t[:, 128 * half : 128 * half + 128]
    copies = []
    for m in range(8):
        parts = [split(mix_ref[half, 256 * m : 256 * m + 256, :]) for half in range(2)]
        hi = jnp.concatenate([p[0] for p in parts], axis=1)
        lo = jnp.concatenate([p[1] for p in parts], axis=1)
        if m == 0:
            for c in loads:
                c.wait()
        both = dot(jnp.concatenate((hi, lo), axis=0), hi_ref[...], 1, 0)
        stage_ref[m] = both[:256] + (both[256:] + dot(hi, lo_ref[...], 1, 0))
        copy = pltpu.make_async_copy(stage_ref.at[m], out_ref.at[pl.ds(256 * m, 256)], sem.at[m])
        copy.start()
        copies.append(copy)
    for copy in copies:
        copy.wait()


def body(recording, source_channels):
    fwd_hi, fwd_lo = (jnp.asarray(t) for t in split_np(forward_table()))
    inv_hi, inv_lo = (jnp.asarray(t) for t in split_np(inverse_table()))
    dma = pltpu.SemaphoreType.DMA
    cross = pl.pallas_call(
        exchange_kernel,
        out_shape=pltpu.VMEM((16, 256, 128), F32),
        in_specs=[HBM] * 4,
        out_specs=VMEM,
        scratch_shapes=[
            pltpu.SMEM((256,), jnp.int32),
            pltpu.VMEM((256, L), F32),
            pltpu.VMEM((256, L), BF),
            pltpu.VMEM((256, L), BF),
            pltpu.VMEM((512, 128), F32),
            pltpu.VMEM((512, 128), F32),
            pltpu.VMEM((2, NZ, 32, 128), F32),
            pltpu.VMEM((NJ, 8, 128), F32),
            pltpu.VMEM((2, 1024, 128), F32),
            pltpu.VMEM((2, 64, 128), F32),
            pltpu.VMEM((3, 64, 128), F32),
            pltpu.VMEM((NJ, 2, 2, 32, 128), F32),
            pltpu.VMEM((2, 32, 16, 128), F32),
            pltpu.VMEM((32, 256, 256), BF),
            dma((4,)), dma, dma((2, NZ)), dma, dma, dma((3,)), dma((3,)), dma, dma, dma, dma((NJ, 2)),
        ],
        compiler_params=pltpu.CompilerParams(collective_id=0, has_side_effects=True),
        name="exchange",
    )(source_channels, recording.reshape(256, L), fwd_hi, fwd_lo)
    out = pl.pallas_call(
        output_kernel,
        out_shape=jax.ShapeDtypeStruct((2048, LAGS), F32),
        in_specs=[VMEM, ANY, ANY],
        out_specs=ANY,
        scratch_shapes=[
            pltpu.VMEM((256, LAGS), BF),
            pltpu.VMEM((256, LAGS), BF),
            pltpu.VMEM((2, 2048, 128), F32),
            pltpu.VMEM((8, 256, LAGS), F32),
            dma((2,)),
            dma((8,)),
        ],
        compiler_params=pltpu.CompilerParams(vmem_limit_bytes=24 << 20),
        name="correlate",
    )(cross, inv_hi, inv_lo)
    return out.reshape(128, 16, LAGS)


def solution(mesh):
    return jax.shard_map(
        body,
        mesh=mesh,
        in_specs=(P("half", "shard", None), P()),
        out_specs=P("half", "shard", None),
        check_vma=False,
    )
```
